256 devices in a mesh: seq: 32 (over z, x_lo, core), head: 8 (over x_hi, y).
Axes of the slice: x: 4 (x_hi: 2, x_lo: 2; x = x_hi * 2 + x_lo), y: 4, z: 8, core: 2. Of those that a mesh axis runs over, the one named last changes fastest.
Arguments:
- tokens: bfloat16 [16384, 2048], P('seq', 'head'), may hold values from -6 to 6
- norm_gain: float32 [2048], replicated, may hold values from 0.25 to 1.75
- w_qkv: bfloat16 [3, 2048, 2048], P(None, None, 'head'), may hold values from -0.125 to 0.125
- head_scale: float32 [16], P('head'), may hold values from 4 to 24
- w_out: bfloat16 [2048, 2048], P('head'), may hold values from -0.25 to 0.25
- scale_ids: int32 [16384], replicated, may hold values from 0 to 9, as said below
Outputs:
- branch_out: bfloat16 [16384, 2048], P('seq', 'head')
The draws below stay inside these ranges and needn't reach their ends.
Inputs may be any that keep to these rules, and one draw needn't show every extreme that they name: scale_ids never falls from one token to the next, and every scale from 0 to 9 occurs.
All inputs are finite; a program needn't handle non-finite values.
Results may differ from the reference program's by a relative error of at most 0.014.
Values may be sent and summed in bfloat16 or wider, within the bound.
A program may use at most 128 MiB of HBM per device.

```python
import math
import jax
import jax.numpy as jnp
from jax import lax

D = 2048
HEADS = 16
HEAD_DIM = 128
NSCALE = 10
TOKENS = 16384


def draw_scale_ids(key, part):
    sizes_table = jnp.array([1, 4, 9, 16, 36, 81, 169, 324, 576, 1024], jnp.int32)
    cumulative = jnp.cumsum(sizes_table)[:-1]
    base = cumulative * TOKENS // 2240
    spread = max(TOKENS // 512, 1)
    jitter = jax.random.randint(key, (NSCALE - 1,), -spread, spread + 1)
    bounds = jnp.clip(base + jitter, 1, TOKENS - NSCALE)
    offsets = jnp.arange(NSCALE - 1, dtype=jnp.int32)
    bounds = lax.cummax(bounds - offsets) + offsets
    position = jnp.arange(TOKENS, dtype=jnp.int32)
    return jnp.sum((position[:, None] >= bounds[None, :]).astype(jnp.int32), axis=1).astype(jnp.int32)


def block_scale(own_key, shape, split, low, top_value):
    factor_of = 1.0
    for dim, shards_of in split:
        steps = jax.random.uniform(jax.random.fold_in(jax.random.fold_in(own_key, 6), dim), (shards_of,), jnp.float32, low / len(split), top_value / len(split))
        factor_of = factor_of * jnp.repeat(jnp.exp(steps), shape[dim] // shards_of).reshape((-1,) + (1,) * (len(shape) - 1 - dim))
    return factor_of


def bell_draw(own_key, extent, scale, reach, pieces=(), kind=jnp.bfloat16):
    values = scale * jax.random.normal(own_key, extent, jnp.float32)
    if pieces:
        values = values * block_scale(own_key, extent, pieces, -0.22, 0.18)
    return jnp.clip(values, -reach, reach).astype(kind)


def setup_inputs(seed: int = 0) -> dict:
    splits = jax.random.split(jax.random.key(seed), 7)
    tokens = bell_draw(splits[0], (TOKENS, D), 1.0, 6.0, ((0, 32), (1, 8)))
    norm_gain = jnp.clip(1.0 + 0.15 * jax.random.normal(splits[1], (D,), jnp.float32), 0.25, 1.75)
    w_qkv = bell_draw(splits[2], (3, D, HEADS * HEAD_DIM), D ** -0.5, 0.125, ((2, 8),))
    head_scale = jnp.clip(jnp.exp(math.log(24.0) - 1.7917595 * jax.random.uniform(splits[3], (HEADS,), jnp.float32) ** block_scale(splits[3], (HEADS,), ((0, 8),), -0.2, 0.2)), 4.0, 24.0)
    w_out = bell_draw(splits[4], (HEADS * HEAD_DIM, D), (HEAD_DIM * 4) ** -0.5, 0.25, ((0, 8),))
    scale_ids = draw_scale_ids(jax.random.fold_in(splits[6], 71), 0)
    return dict(tokens=tokens, norm_gain=norm_gain, w_qkv=w_qkv, head_scale=head_scale, w_out=w_out, scale_ids=scale_ids)


def rms_normed(tokens, norm_gain):
    values = tokens.astype(jnp.float32)
    power = lax.optimization_barrier(jnp.mean(values * values, axis=-1, keepdims=True))
    return (values * lax.rsqrt(power + 1e-06) * norm_gain).astype(jnp.bfloat16)

def unit_rows(values, factor):
    power = lax.optimization_barrier(jnp.sum(values * values, axis=-1, keepdims=True))
    return (values * lax.rsqrt(power + 1e-06) * factor).astype(jnp.bfloat16)

def reference(tokens, norm_gain, w_qkv, head_scale, w_out, scale_ids):
    count = tokens.shape[0]
    normed = rms_normed(tokens, norm_gain)
    query = jnp.dot(normed, w_qkv[0], preferred_element_type=jnp.float32).reshape(count, HEADS, HEAD_DIM)
    keyset = jnp.dot(normed, w_qkv[1], preferred_element_type=jnp.float32).reshape(count, HEADS, HEAD_DIM)
    valset = jnp.dot(normed, w_qkv[2], preferred_element_type=jnp.float32).reshape(count, HEADS, HEAD_DIM)
    query_n = unit_rows(query, head_scale[None, :, None])
    key_n = unit_rows(keyset, 1.0).astype(jnp.float32)
    val_b = valset.astype(jnp.bfloat16).astype(jnp.float32)
    block = min(128, count)
    query_blocks = query_n.reshape(count // block, block, HEADS, HEAD_DIM)
    id_blocks = scale_ids.reshape(count // block, block)

    def one_block(args):
        qblk, qid = args
        score = jnp.einsum('qhd,khd->hqk', qblk.astype(jnp.float32), key_n)
        allowed = (scale_ids[None, :] <= qid[:, None])[None]
        score = jnp.where(allowed, score, -1e+30)
        top = lax.optimization_barrier(jnp.max(score, axis=-1, keepdims=True))
        expo = jnp.where(allowed, jnp.exp(score - top), 0.0)
        total = lax.optimization_barrier(jnp.sum(expo, axis=-1))
        weight = expo.astype(jnp.bfloat16).astype(jnp.float32)
        summed = jnp.einsum('hqk,khd->qhd', weight, val_b)
        return summed / jnp.transpose(total)[:, :, None]
    attended = lax.map(one_block, (query_blocks, id_blocks))
    attended = attended.reshape(count, HEADS * HEAD_DIM).astype(jnp.bfloat16)
    return jnp.dot(attended, w_out, preferred_element_type=jnp.float32).astype(jnp.bfloat16)
```

```python
import functools
import math

import jax
import jax.numpy as jnp
from jax import lax
from jax.experimental import pallas as pl
from jax.experimental.pallas import tpu as pltpu
from jax.sharding import PartitionSpec as P

MESH = pl.DeviceIdType.MESH
BF = jnp.bfloat16
F32 = jnp.float32
LOG2E = math.log2(math.e)


def kernel(
    tokens, gain, wqkv, hscale, wout, ids, out,
    xg, wq, acc3, ssq, kv, kvsend, qbuf, qsend, qid, oacc, lacc, attg, osend, wc,
    lsem, gs_x, gr_x, gs_y, gr_y, as_x, ar_x, as_y, ar_y, ws, wr, xs, xr, zs, zr, cs, cr,
):
    rows, feat = tokens.shape
    hd_dim = 128
    sid = lax.axis_index("seq")
    hid = lax.axis_index("head")
    z, xl, c = sid // 4, (sid // 2) % 2, sid % 2
    xh, y = hid // 4, hid % 4

    def sq(zz, xx, cc):
        return lax.rem(zz + 8, 8) * 4 + xx * 2 + cc

    def hx(xx, yy):
        return xx * 4 + lax.rem(yy + 4, 4)

    def at_head(h):
        return (sid, h)

    def at_seq(s):
        return (s, hid)

    x_partner = at_head(hx(1 - xh, y))
    y_up, y_down = at_head(hx(xh, y + 1)), at_head(hx(xh, y - 1))
    pair = at_seq(sq(z, 1 - xl, c))
    twin = at_seq(sq(z, xl, 1 - c))
    z_up, z_down = at_seq(sq(z + 1, xl, c)), at_seq(sq(z - 1, xl, c))

    def remote(src, dst, ssem, rsem, dev):
        return pltpu.make_async_remote_copy(
            src_ref=src, dst_ref=dst, send_sem=ssem, recv_sem=rsem, device_id=dev, device_id_type=MESH
        )

    own = pltpu.make_async_copy(tokens, xg.at[hid], lsem.at[0])
    own.start()
    loads = pltpu.make_async_copy(wqkv, wq, lsem.at[1])
    loads.start()
    own_w = pltpu.make_async_copy(wout.at[:, pl.ds(pl.multiple_of(hid * feat, feat), feat)], wc.at[hid], lsem.at[2])
    own_w.start()

    barrier = pltpu.get_barrier_semaphore()
    for d in range(1, 8):
        pl.semaphore_signal(barrier, inc=1, device_id=at_head(lax.rem(hid + d, 8)), device_id_type=MESH)
    for dev in (pair, twin, z_up, z_down):
        pl.semaphore_signal(barrier, inc=1, device_id=dev, device_id_type=MESH)
    pl.semaphore_wait(barrier, 11)

    pending = []

    def go(copy):
        copy.start()
        pending.append(copy)
        return copy

    def gather(first, buf, sx, rx, sy, ry, consume):
        mine, other = hx(xh, y), hx(1 - xh, y)
        half = rows // 2
        top, bottom = pl.ds(0, half), pl.ds(half, half)
        go(remote(first, buf.at[mine], sx.at[0], rx.at[0], x_partner))
        go(remote(first, buf.at[mine], sy.at[0], ry.at[0], y_up))
        go(remote(first, buf.at[mine], sy.at[1], ry.at[1], y_down))
        remote(first, buf.at[other], sx.at[0], rx.at[0], x_partner).wait_recv()
        go(remote(buf.at[other], buf.at[other], sy.at[2], ry.at[2], y_up))
        go(remote(buf.at[other], buf.at[other], sy.at[3], ry.at[3], y_down))
        for g, xx in ((0, xh), (1, 1 - xh)):
            lo, hi = hx(xx, y - 1), hx(xx, y + 1)
            if g == 0:
                consume(0)
            remote(buf.at[lo], buf.at[lo], sy.at[0], ry.at[2 * g], y_up).wait_recv()
            go(remote(buf.at[lo, top], buf.at[lo, top], sy.at[4 + 2 * g], ry.at[4 + 2 * g], y_up))
            remote(buf.at[hi], buf.at[hi], sy.at[0], ry.at[2 * g + 1], y_down).wait_recv()
            go(remote(buf.at[hi, bottom], buf.at[hi, bottom], sy.at[5 + 2 * g], ry.at[5 + 2 * g], y_down))
            consume(1 + g)
        for g, xx in ((0, xh), (1, 1 - xh)):
            far = hx(xx, y + 2)
            remote(buf.at[far, top], buf.at[far, top], sy.at[4], ry.at[4 + 2 * g], y_up).wait_recv()
            remote(buf.at[far, bottom], buf.at[far, bottom], sy.at[5], ry.at[5 + 2 * g], y_down).wait_recv()
        consume(3)

    def piece_of(stage, i):
        if stage == 0:
            return lax.rem(xh + i, 2) * 4 + y
        if stage == 3:
            return lax.rem(xh + i, 2) * 4 + lax.rem(y + 2, 4)
        g = stage - 1
        return lax.rem(xh + g, 2) * 4 + lax.rem(y + 3 + 2 * i, 4)

    for i in range(2):
        for j in range(4):
            row = ids[pl.ds(sq(z, i, c) * 4 + j, 1), :]
            qid[i, pl.ds(j * 128, 128), :] = jnp.broadcast_to(row.astype(F32), (128, 128)).T
    oacc[...] = jnp.zeros_like(oacc)
    lacc[...] = jnp.zeros_like(lacc)
    acc3[...] = jnp.zeros_like(acc3)
    ssq[...] = jnp.zeros_like(ssq)
    own.wait()
    loads.wait()

    def project(stage):
        def body(i, carry):
            p = piece_of(stage, i)
            lane = pl.ds(pl.multiple_of(p * feat, feat), feat)
            x = xg[p].astype(F32)
            sqv = x * x
            ssq[...] += sqv[:, :128] + sqv[:, 128:]
            xw = (x * gain[:, lane]).astype(BF)
            for j in range(3):
                acc3[:, j * feat:(j + 1) * feat] += jnp.dot(xw, wq[j, lane, :], preferred_element_type=F32)
            return carry

        lax.fori_loop(0, 2, body, 0)

    gather(tokens, xg, gs_x, gr_x, gs_y, gr_y, project)

    r = lax.rsqrt(jnp.sum(ssq[...], axis=-1, keepdims=True) * (1.0 / (8 * feat)) + 1e-06)

    def head_of(j, h):
        return acc3[:, pl.ds(pl.multiple_of(j * feat + h * hd_dim, hd_dim), hd_dim)] * r

    def unit(v, factor):
        power = jnp.sum(v * v, axis=-1, keepdims=True)
        return (v * lax.rsqrt(power + 1e-06) * factor).astype(BF)

    kv[sid, 0] = unit(head_of(1, xl), 1.0)
    kv[sid, 1] = head_of(2, xl).astype(BF)
    go(remote(kv.at[sid], kv.at[sid], zs.at[0, 0], zr.at[0, 0], z_up))
    go(remote(kv.at[sid], kv.at[sid], zs.at[1, 0], zr.at[1, 0], z_down))
    go(remote(kv.at[sid], kv.at[sid], cs.at[2, 0], cr.at[2, 0], twin))
    kvsend[0] = unit(head_of(1, 1 - xl), 1.0)
    kvsend[1] = head_of(2, 1 - xl).astype(BF)
    go(remote(kvsend, kv.at[sid], xs.at[0], xr.at[0], pair))
    qsend[...] = unit(head_of(0, 1 - xl), hscale[0, 1 - xl] * LOG2E)
    go(remote(qsend, qbuf.at[xl], xs.at[1], xr.at[1], pair))
    qbuf[xl] = unit(head_of(0, xl), hscale[0, xl] * LOG2E)
    other = sq(z, 1 - xl, c)
    remote(kvsend, kv.at[other], xs.at[0], xr.at[0], pair).wait_recv()
    go(remote(kv.at[other], kv.at[other], zs.at[0, 1], zr.at[0, 1], z_up))
    go(remote(kv.at[other], kv.at[other], zs.at[1, 1], zr.at[1, 1], z_down))
    go(remote(kv.at[other], kv.at[other], cs.at[2, 1], cr.at[2, 1], twin))

    for d in range(1, 8):
        to = lax.rem(hid + d, 8)
        go(remote(
            wout.at[:, pl.ds(pl.multiple_of(to * feat, feat), feat)], wc.at[hid],
            ws.at[d], wr.at[d], at_head(to),
        ))
    remote(qsend, qbuf.at[1 - xl], xs.at[1], xr.at[1], pair).wait_recv()

    qrows = 256

    def attend(blk):
        k, v = kv[blk, 0], kv[blk, 1]
        kids = [ids[pl.ds(blk * 4 + j, 1), :].astype(F32) for j in range(4)]
        for qb in range(2 * rows // qrows):
            i, lo = divmod(qb * qrows, rows)
            q = qbuf[i, pl.ds(lo, qrows), :]
            s = lax.dot_general(q, k, (((1,), (1,)), ((), ())), preferred_element_type=F32)
            qi = qid[i, pl.ds(lo, qrows), :]
            parts = []
            total = None
            for j in range(4):
                e = jnp.where(kids[j] <= qi, jnp.exp2(s[:, j * 128:(j + 1) * 128]), 0.0)
                total = e if total is None else total + e
                parts.append(e.astype(BF))
            w = jnp.concatenate(parts, axis=1)
            span = pl.ds(lo, qrows)
            oacc[i, span, :] += jnp.dot(w, v, preferred_element_type=F32)
            lacc[i, span, :] += total

    def block_at(dz, u, cc):
        return lax.rem(z + dz + 8, 8) * 4 + lax.rem(xl + u, 2) * 2 + cc

    def loop2(f):
        lax.fori_loop(0, 2, lambda i, carry: (f(i), carry)[1], 0)

    def ring(k, d, dev_step):
        s, u = k // 2 + 1, lax.rem(k, 2)
        blk = block_at(-s if d == 0 else s, u, c)
        remote(kv.at[blk], kv.at[blk], zs.at[d, 0], zr.at[d, k], z_up).wait_recv()
        return blk

    def to_twin(blk, d, k):
        return remote(kv.at[blk], kv.at[blk], cs.at[d, k], cr.at[d, k], twin)

    def from_twin(blk, d, k):
        remote(kv.at[blk], kv.at[blk], cs.at[d, 0], cr.at[d, k], twin).wait_recv()

    loop2(lambda i: attend(block_at(0, i, c)))
    from_twin(block_at(0, 0, 1 - c), 2, 0)
    from_twin(block_at(0, 1, 1 - c), 2, 1)
    loop2(lambda i: attend(block_at(0, i, 1 - c)))

    def lagged(k):
        s, u = k // 2 + 1, lax.rem(k, 2)
        from_twin(block_at(-s, u, 1 - c), 0, k)
        from_twin(block_at(s, u, 1 - c), 1, k)
        loop2(lambda i: attend(block_at((2 * i - 1) * s, u, 1 - c)))

    def period(p, carry):
        s, u = p // 2 + 1, lax.rem(p, 2)
        up = ring(p, 0, z_up)

        @pl.when(p <= 4)
        def _():
            remote(kv.at[up], kv.at[up], zs.at[0, p + 2], zr.at[0, p + 2], z_up).start()

        to_twin(up, 0, p).start()
        down = ring(p, 1, z_down)

        @pl.when(p <= 3)
        def _():
            remote(kv.at[down], kv.at[down], zs.at[1, p + 2], zr.at[1, p + 2], z_down).start()

        @pl.when(p == 5)
        def _():
            remote(kv.at[down], kv.at[down], zs.at[1, p + 2], zr.at[1, p + 2], z_down).start()

        to_twin(down, 1, p).start()
        loop2(lambda i: attend(block_at((2 * i - 1) * s, u, c)))

        @pl.when(p > 0)
        def _():
            lagged(p - 1)

        return carry

    lax.fori_loop(0, 6, period, 0)
    lagged(5)
    last_up = block_at(4, 0, c)
    last_down = block_at(4, 1, c)
    remote(kv.at[last_up], kv.at[last_up], zs.at[0, 0], zr.at[0, 6], z_up).wait_recv()
    go(to_twin(last_up, 0, 6))
    remote(kv.at[last_down], kv.at[last_down], zs.at[1, 0], zr.at[1, 7], z_up).wait_recv()
    go(to_twin(last_down, 1, 7))
    loop2(lambda i: attend(block_at(4, i, c)))
    from_twin(block_at(4, 0, 1 - c), 0, 6)
    from_twin(block_at(4, 1, 1 - c), 1, 7)
    loop2(lambda i: attend(block_at(4, i, 1 - c)))

    def attended(i):
        total = jnp.sum(lacc[i], axis=-1, keepdims=True)
        return (oacc[i] / total).astype(BF)

    osend[...] = attended(1 - xl)
    go(remote(osend, attg.at[hid, xl], xs.at[2], xr.at[2], pair))
    attg[hid, xl] = attended(xl)
    remote(osend, attg.at[hid, 1 - xl], xs.at[2], xr.at[2], pair).wait_recv()

    own_w.wait()
    for d in range(1, 8):
        frm = lax.rem(hid - d + 8, 8)
        remote(wc.at[frm], wc.at[frm], ws.at[d], wr.at[d], at_head(frm)).wait_recv()

    fin = acc3.at[:, pl.ds(0, feat)]

    def finish(stage):
        def body(i, carry):
            p = piece_of(stage, i)
            a = jnp.concatenate([attg[p, 0], attg[p, 1]], axis=1)
            d = jnp.dot(a, wc[p], preferred_element_type=F32)
            fin[...] += d
            return carry

        lax.fori_loop(0, 2, body, 0)

    fin[...] = jnp.zeros((rows, feat), F32)
    gather2(remote, go, attg, hid, hx, xh, y, x_partner, y_up, y_down, as_x, ar_x, as_y, ar_y, finish)
    out[...] = fin[...].astype(BF)

    for k in range(2, 7):
        remote(kv.at[0], kv.at[0], zs.at[0, k], zr.at[0, 0], z_up).wait_send()
    for k in (2, 3, 4, 5, 7):
        remote(kv.at[0], kv.at[0], zs.at[1, k], zr.at[1, 0], z_down).wait_send()
    for k in range(6):
        for d in range(2):
            remote(kv.at[0], kv.at[0], cs.at[d, k], cr.at[d, 0], twin).wait_send()
    for copy in pending:
        copy.wait_send()


def gather2(remote, go, buf, hid, hx, xh, y, x_partner, y_up, y_down, sx, rx, sy, ry, consume):
    mine, other = hx(xh, y), hx(1 - xh, y)
    go(remote(buf.at[mine], buf.at[mine], sx.at[0], rx.at[0], x_partner))
    go(remote(buf.at[mine], buf.at[mine], sy.at[0], ry.at[0], y_up))
    go(remote(buf.at[mine], buf.at[mine], sy.at[1], ry.at[1], y_down))
    remote(buf.at[other], buf.at[other], sx.at[0], rx.at[0], x_partner).wait_recv()
    go(remote(buf.at[other], buf.at[other], sy.at[2], ry.at[2], y_up))
    go(remote(buf.at[other], buf.at[other], sy.at[3], ry.at[3], y_down))
    for g, xx in ((0, xh), (1, 1 - xh)):
        lo, hi = hx(xx, y - 1), hx(xx, y + 1)
        if g == 0:
            consume(0)
        remote(buf.at[lo], buf.at[lo], sy.at[0], ry.at[2 * g], y_up).wait_recv()
        go(remote(buf.at[lo, 0], buf.at[lo, 0], sy.at[4 + 2 * g], ry.at[4 + 2 * g], y_up))
        remote(buf.at[hi], buf.at[hi], sy.at[0], ry.at[2 * g + 1], y_down).wait_recv()
        go(remote(buf.at[hi, 1], buf.at[hi, 1], sy.at[5 + 2 * g], ry.at[5 + 2 * g], y_down))
        consume(1 + g)
    for g, xx in ((0, xh), (1, 1 - xh)):
        far = hx(xx, y + 2)
        remote(buf.at[far, 0], buf.at[far, 0], sy.at[4], ry.at[4 + 2 * g], y_up).wait_recv()
        remote(buf.at[far, 1], buf.at[far, 1], sy.at[5], ry.at[5 + 2 * g], y_down).wait_recv()
    consume(3)


def body(tokens, norm_gain, w_qkv, head_scale, w_out, scale_ids):
    rows, feat = tokens.shape
    dim = w_qkv.shape[1]
    dma = pltpu.SemaphoreType.DMA
    any_spec = pl.BlockSpec(memory_space=pl.ANY)
    vm = pl.BlockSpec(memory_space=pltpu.VMEM)
    return pl.pallas_call(
        kernel,
        name="branch",
        out_shape=jax.ShapeDtypeStruct((rows, feat), BF),
        in_specs=[any_spec, vm, any_spec, pl.BlockSpec(memory_space=pltpu.SMEM), any_spec, vm],
        out_specs=vm,
        scratch_shapes=[
            pltpu.VMEM((8, rows, feat), BF),
            pltpu.VMEM((3, dim, feat), BF),
            pltpu.VMEM((rows, 3 * feat), F32),
            pltpu.VMEM((rows, 128), F32),
            pltpu.VMEM((32, 2, rows, 128), BF),
            pltpu.VMEM((2, rows, 128), BF),
            pltpu.VMEM((2, rows, 128), BF),
            pltpu.VMEM((rows, 128), BF),
            pltpu.VMEM((2, rows, 128), F32),
            pltpu.VMEM((2, rows, 128), F32),
            pltpu.VMEM((2, rows, 128), F32),
            pltpu.VMEM((8, 2, rows, 128), BF),
            pltpu.VMEM((rows, 128), BF),
            pltpu.VMEM((8, feat, feat), BF),
            dma((3,)),
            dma((1,)), dma((1,)), dma((8,)), dma((8,)),
            dma((1,)), dma((1,)), dma((8,)), dma((8,)),
            dma((8,)), dma((8,)),
            dma((3,)), dma((3,)),
            dma((2, 8)), dma((2, 8)),
            dma((3, 8)), dma((3, 8)),
        ],
        compiler_params=pltpu.CompilerParams(
            collective_id=0, has_side_effects=True, vmem_limit_bytes=56 * 1024 * 1024
        ),
        cost_estimate=pl.CostEstimate(flops=11_000_000_000, bytes_accessed=6_000_000, transcendentals=17_000_000),
    )(tokens, norm_gain.reshape(1, -1), w_qkv, head_scale.reshape(1, -1), w_out, scale_ids.reshape(-1, 128))


def solution(mesh):
    placed = (P("seq", "head"), P(), P(None, None, "head"), P("head"), P("head", None), P())
    return jax.shard_map(
        body, mesh=mesh, in_specs=placed, out_specs=P("seq", "head"), check_vma=False
    )
```

```python
import functools
import math

import jax
import jax.numpy as jnp
from jax import lax
from jax.experimental import pallas as pl
from jax.experimental.pallas import tpu as pltpu
from jax.sharding import PartitionSpec as P

MESH = pl.DeviceIdType.MESH
BF = jnp.bfloat16
F32 = jnp.float32
LOG2E = math.log2(math.e)


def kernel(
    tokens, gain, wqkv, hscale, wout, ids, out,
    xg, wq, acc3, ssq, kv, kvsend, qbuf, qsend, qid, oacc, lacc, attg, osend, wc,
    lsem, gs_x, gr_x, gs_y, gr_y, os, orr, ys, yr, ws, wr, xs, xr, zs, zr, cs, cr,
):
    rows, feat = tokens.shape
    hd_dim = 128
    sid = lax.axis_index("seq")
    hid = lax.axis_index("head")
    z, xl, c = sid // 4, (sid // 2) % 2, sid % 2
    xh, y = hid // 4, hid % 4

    def sq(zz, xx, cc):
        return lax.rem(zz + 8, 8) * 4 + xx * 2 + cc

    def hx(xx, yy):
        return xx * 4 + lax.rem(yy + 4, 4)

    def at_head(h):
        return (sid, h)

    def at_seq(s):
        return (s, hid)

    x_partner = at_head(hx(1 - xh, y))
    y_up, y_down = at_head(hx(xh, y + 1)), at_head(hx(xh, y - 1))
    pair = at_seq(sq(z, 1 - xl, c))
    twin = at_seq(sq(z, xl, 1 - c))
    diag = (sq(z, 1 - xl, c), hx(1 - xh, y))
    z_up, z_down = at_seq(sq(z + 1, xl, c)), at_seq(sq(z - 1, xl, c))

    def remote(src, dst, ssem, rsem, dev):
        return pltpu.make_async_remote_copy(
            src_ref=src, dst_ref=dst, send_sem=ssem, recv_sem=rsem, device_id=dev, device_id_type=MESH
        )

    own = pltpu.make_async_copy(tokens, xg.at[hid], lsem.at[0])
    own.start()
    loads = pltpu.make_async_copy(wqkv, wq, lsem.at[1])
    loads.start()
    own_w = pltpu.make_async_copy(wout.at[:, pl.ds(pl.multiple_of(hid * feat, feat), feat)], wc.at[hid], lsem.at[2])
    own_w.start()

    barrier = pltpu.get_barrier_semaphore()
    for d in range(1, 8):
        pl.semaphore_signal(barrier, inc=1, device_id=at_head(lax.rem(hid + d, 8)), device_id_type=MESH)
    for dev in (pair, twin, diag, z_up, z_down):
        pl.semaphore_signal(barrier, inc=1, device_id=dev, device_id_type=MESH)
    pl.semaphore_wait(barrier, 12)

    pending = []

    def go(copy):
        copy.start()
        pending.append(copy)
        return copy

    def gather(first, buf, sx, rx, sy, ry, consume):
        mine, other = hx(xh, y), hx(1 - xh, y)
        half = rows // 2
        top, bottom = pl.ds(0, half), pl.ds(half, half)
        go(remote(first, buf.at[mine], sx.at[0], rx.at[0], x_partner))
        go(remote(first, buf.at[mine], sy.at[0], ry.at[0], y_up))
        go(remote(first, buf.at[mine], sy.at[1], ry.at[1], y_down))
        remote(first, buf.at[other], sx.at[0], rx.at[0], x_partner).wait_recv()
        go(remote(buf.at[other], buf.at[other], sy.at[2], ry.at[2], y_up))
        go(remote(buf.at[other], buf.at[other], sy.at[3], ry.at[3], y_down))
        for g, xx in ((0, xh), (1, 1 - xh)):
            lo, hi = hx(xx, y - 1), hx(xx, y + 1)
            if g == 0:
                consume(0)
            remote(buf.at[lo], buf.at[lo], sy.at[0], ry.at[2 * g], y_up).wait_recv()
            go(remote(buf.at[lo, top], buf.at[lo, top], sy.at[4 + 2 * g], ry.at[4 + 2 * g], y_up))
            remote(buf.at[hi], buf.at[hi], sy.at[0], ry.at[2 * g + 1], y_down).wait_recv()
            go(remote(buf.at[hi, bottom], buf.at[hi, bottom], sy.at[5 + 2 * g], ry.at[5 + 2 * g], y_down))
            consume(1 + g)
        for g, xx in ((0, xh), (1, 1 - xh)):
            far = hx(xx, y + 2)
            remote(buf.at[far, top], buf.at[far, top], sy.at[4], ry.at[4 + 2 * g], y_up).wait_recv()
            remote(buf.at[far, bottom], buf.at[far, bottom], sy.at[5], ry.at[5 + 2 * g], y_down).wait_recv()
        consume(3)

    def piece_of(stage, i):
        if stage == 0:
            return lax.rem(xh + i, 2) * 4 + y
        if stage == 3:
            return lax.rem(xh + i, 2) * 4 + lax.rem(y + 2, 4)
        g = stage - 1
        return lax.rem(xh + g, 2) * 4 + lax.rem(y + 3 + 2 * i, 4)

    for i in range(2):
        for j in range(4):
            row = ids[pl.ds(sq(z, i, c) * 4 + j, 1), :]
            qid[i, pl.ds(j * 128, 128), :] = jnp.broadcast_to(row.astype(F32), (128, 128)).T
    oacc[...] = jnp.zeros_like(oacc)
    lacc[...] = jnp.zeros_like(lacc)
    acc3[...] = jnp.zeros_like(acc3)
    ssq[...] = jnp.zeros_like(ssq)
    own.wait()
    loads.wait()

    def project(stage):
        def body(i, carry):
            p = piece_of(stage, i)
            lane = pl.ds(pl.multiple_of(p * feat, feat), feat)
            x = xg[p].astype(F32)
            sqv = x * x
            ssq[...] += sqv[:, :128] + sqv[:, 128:]
            xw = (x * gain[:, lane]).astype(BF)
            for j in range(3):
                acc3[:, j * feat:(j + 1) * feat] += jnp.dot(xw, wq[j, lane, :], preferred_element_type=F32)
            return carry

        lax.fori_loop(0, 2, body, 0)

    gather(tokens, xg, gs_x, gr_x, gs_y, gr_y, project)

    r = lax.rsqrt(jnp.sum(ssq[...], axis=-1, keepdims=True) * (1.0 / (8 * feat)) + 1e-06)

    def head_of(j, h):
        return acc3[:, pl.ds(pl.multiple_of(j * feat + h * hd_dim, hd_dim), hd_dim)] * r

    def unit(v, factor):
        power = jnp.sum(v * v, axis=-1, keepdims=True)
        return (v * lax.rsqrt(power + 1e-06) * factor).astype(BF)

    half = rows // 2

    def store(dst, j, value):
        dst[0, j] = value[:half]
        dst[1, j] = value[half:]

    store(kv.at[sid], 0, unit(head_of(1, xl), 1.0))
    store(kv.at[sid], 1, head_of(2, xl).astype(BF))
    go(remote(kv.at[sid], kv.at[sid], zs.at[0, 0], zr.at[0, 0], z_up))
    go(remote(kv.at[sid], kv.at[sid], zs.at[1, 0], zr.at[1, 0], z_down))
    go(remote(kv.at[sid], kv.at[sid], cs.at[2, 0], cr.at[2, 0], twin))
    store(kvsend, 0, unit(head_of(1, 1 - xl), 1.0))
    store(kvsend, 1, head_of(2, 1 - xl).astype(BF))
    go(remote(kvsend, kv.at[sid], xs.at[0], xr.at[0], pair))
    qsend[...] = unit(head_of(0, 1 - xl), hscale[0, 1 - xl] * LOG2E)
    go(remote(qsend, qbuf.at[xl], xs.at[1], xr.at[1], pair))
    qbuf[xl] = unit(head_of(0, xl), hscale[0, xl] * LOG2E)
    other = sq(z, 1 - xl, c)
    remote(kvsend, kv.at[other], xs.at[0], xr.at[0], pair).wait_recv()
    go(remote(kv.at[other], kv.at[other], zs.at[0, 1], zr.at[0, 1], z_up))
    go(remote(kv.at[other], kv.at[other], zs.at[1, 1], zr.at[1, 1], z_down))
    go(remote(kv.at[other], kv.at[other], cs.at[2, 1], cr.at[2, 1], twin))

    for d in range(1, 8):
        to = lax.rem(hid + d, 8)
        go(remote(
            wout.at[:, pl.ds(pl.multiple_of(to * feat, feat), feat)], wc.at[hid],
            ws.at[d], wr.at[d], at_head(to),
        ))
    remote(qsend, qbuf.at[1 - xl], xs.at[1], xr.at[1], pair).wait_recv()

    def attend(blk, parts_of=(0, 1)):
        k = jnp.concatenate([kv[blk, 0, 0], kv[blk, 1, 0]], axis=0)
        v = jnp.concatenate([kv[blk, 0, 1], kv[blk, 1, 1]], axis=0)
        kids = [ids[pl.ds(blk * 4 + j, 1), :].astype(F32) for j in range(4)]
        for qh in parts_of:
            for i in range(2):
                span = pl.ds(qh * half, half)
                q = qbuf[i, span, :]
                s = lax.dot_general(q, k, (((1,), (1,)), ((), ())), preferred_element_type=F32)
                qi = qid[i, span, :]
                parts = []
                total = None
                for j in range(4):
                    e = jnp.where(kids[j] <= qi, jnp.exp2(s[:, j * 128:(j + 1) * 128]), 0.0)
                    total = e if total is None else total + e
                    parts.append(e.astype(BF))
                w = jnp.concatenate(parts, axis=1)
                oacc[i, span, :] += jnp.dot(w, v, preferred_element_type=F32)
                lacc[i, span, :] += total

    def block_at(dz, u, cc):
        return lax.rem(z + dz + 8, 8) * 4 + lax.rem(xl + u, 2) * 2 + cc

    def loop2(f):
        lax.fori_loop(0, 2, lambda i, carry: (f(i), carry)[1], 0)

    def ring(k, d, dev_step):
        s, u = k // 2 + 1, lax.rem(k, 2)
        blk = block_at(-s if d == 0 else s, u, c)
        remote(kv.at[blk], kv.at[blk], zs.at[d, 0], zr.at[d, k], z_up).wait_recv()
        return blk

    def to_twin(blk, d, k):
        return remote(kv.at[blk], kv.at[blk], cs.at[d, k], cr.at[d, k], twin)

    def from_twin(blk, d, k):
        remote(kv.at[blk], kv.at[blk], cs.at[d, 0], cr.at[d, k], twin).wait_recv()

    loop2(lambda i: attend(block_at(0, i, c)))
    from_twin(block_at(0, 0, 1 - c), 2, 0)
    from_twin(block_at(0, 1, 1 - c), 2, 1)
    loop2(lambda i: attend(block_at(0, i, 1 - c)))

    def lagged(k):
        s, u = k // 2 + 1, lax.rem(k, 2)
        from_twin(block_at(-s, u, 1 - c), 0, k)
        from_twin(block_at(s, u, 1 - c), 1, k)
        loop2(lambda i: attend(block_at((2 * i - 1) * s, u, 1 - c)))

    def period(p, carry):
        s, u = p // 2 + 1, lax.rem(p, 2)
        up = ring(p, 0, z_up)

        @pl.when(p <= 4)
        def _():
            remote(kv.at[up], kv.at[up], zs.at[0, p + 2], zr.at[0, p + 2], z_up).start()

        to_twin(up, 0, p).start()
        down = ring(p, 1, z_down)

        @pl.when(p <= 3)
        def _():
            remote(kv.at[down], kv.at[down], zs.at[1, p + 2], zr.at[1, p + 2], z_down).start()

        @pl.when(p == 5)
        def _():
            remote(kv.at[down], kv.at[down], zs.at[1, p + 2], zr.at[1, p + 2], z_down).start()

        to_twin(down, 1, p).start()
        loop2(lambda i: attend(block_at((2 * i - 1) * s, u, c)))

        @pl.when(p > 0)
        def _():
            lagged(p - 1)

        return carry

    lax.fori_loop(0, 6, period, 0)
    lagged(5)
    last_up = block_at(4, 0, c)
    last_down = block_at(4, 1, c)
    remote(kv.at[last_up], kv.at[last_up], zs.at[0, 0], zr.at[0, 6], z_up).wait_recv()
    go(to_twin(last_up, 0, 6))
    remote(kv.at[last_down], kv.at[last_down], zs.at[1, 0], zr.at[1, 7], z_up).wait_recv()
    go(to_twin(last_down, 1, 7))
    oid = hx(1 - xh, y)

    def hand_out(qh):
        span = pl.ds(qh * half, half)

        def attended(i):
            total = jnp.sum(lacc[i, span, :], axis=-1, keepdims=True)
            return (oacc[i, span, :] / total).astype(BF)

        osend[qh] = attended(1 - xl)
        mine = attg.at[hid, qh, xl]
        go(remote(osend.at[qh], mine, os.at[qh, 0], orr.at[qh, 0], pair))
        go(remote(osend.at[qh], mine, os.at[qh, 1], orr.at[qh, 1], diag))
        attg[hid, qh, xl] = attended(xl)
        go(remote(mine, mine, os.at[qh, 2], orr.at[qh, 2], x_partner))

    loop2(lambda i: attend(block_at(4, i, c), (0,)))
    from_twin(block_at(4, 0, 1 - c), 0, 6)
    from_twin(block_at(4, 1, 1 - c), 1, 7)
    loop2(lambda i: attend(block_at(4, i, 1 - c), (0,)))
    hand_out(0)

    def last(i, carry):
        attend(lax.rem(z + 4, 8) * 4 + lax.rem(xl + i, 2) * 2 + lax.rem(c + i // 2, 2), (1,))
        return carry

    lax.fori_loop(0, 4, last, 0)
    hand_out(1)

    own_w.wait()
    for d in range(1, 8):
        frm = lax.rem(hid - d + 8, 8)
        remote(wc.at[frm], wc.at[frm], ws.at[d], wr.at[d], at_head(frm)).wait_recv()

    fin = acc3.at[:, pl.ds(0, feat)]
    fin[...] = jnp.zeros((rows, feat), F32)

    def finish(stage, qh):
        def step(i, carry):
            p = piece_of(stage, i)
            a = jnp.concatenate([attg[p, qh, 0], attg[p, qh, 1]], axis=1)
            fin[pl.ds(qh * half, half), :] += jnp.dot(a, wc[p], preferred_element_type=F32)
            return carry

        lax.fori_loop(0, 2, step, 0)

    for qh in range(2):
        slot = attg.at[hid, qh, 1 - xl]
        remote(slot, slot, os.at[qh, 0], orr.at[qh, 0], pair).wait_recv()
        whole = attg.at[hid, qh]
        go(remote(whole, whole, ys.at[qh, 0], yr.at[qh, 0], y_up))
        go(remote(whole, whole, ys.at[qh, 1], yr.at[qh, 1], y_down))
        slot = attg.at[oid, qh, 1 - xl]
        remote(slot, slot, os.at[qh, 1], orr.at[qh, 1], diag).wait_recv()
        slot = attg.at[oid, qh, xl]
        remote(slot, slot, os.at[qh, 2], orr.at[qh, 2], x_partner).wait_recv()
        whole = attg.at[oid, qh]
        go(remote(whole, whole, ys.at[qh, 2], yr.at[qh, 2], y_up))
        go(remote(whole, whole, ys.at[qh, 3], yr.at[qh, 3], y_down))
    finish(0, 0)
    finish(0, 1)
    for qh in range(2):
        for g, xx in ((0, xh), (1, 1 - xh)):
            lo, hi = attg.at[hx(xx, y - 1), qh], attg.at[hx(xx, y + 1), qh]
            remote(lo, lo, ys.at[qh, 0], yr.at[qh, 2 * g], y_up).wait_recv()
            go(remote(lo.at[0], lo.at[0], ys.at[qh, 4 + 2 * g], yr.at[qh, 4 + 2 * g], y_up))
            remote(hi, hi, ys.at[qh, 1], yr.at[qh, 2 * g + 1], y_down).wait_recv()
            go(remote(hi.at[1], hi.at[1], ys.at[qh, 5 + 2 * g], yr.at[qh, 5 + 2 * g], y_down))
            finish(1 + g, qh)
    for qh in range(2):
        for g, xx in ((0, xh), (1, 1 - xh)):
            far = attg.at[hx(xx, y + 2), qh]
            remote(far.at[0], far.at[0], ys.at[qh, 4], yr.at[qh, 4 + 2 * g], y_up).wait_recv()
            remote(far.at[1], far.at[1], ys.at[qh, 5], yr.at[qh, 5 + 2 * g], y_down).wait_recv()
        finish(3, qh)
    out[...] = fin[...].astype(BF)

    for k in range(2, 7):
        remote(kv.at[0], kv.at[0], zs.at[0, k], zr.at[0, 0], z_up).wait_send()
    for k in (2, 3, 4, 5, 7):
        remote(kv.at[0], kv.at[0], zs.at[1, k], zr.at[1, 0], z_down).wait_send()
    for k in range(6):
        for d in range(2):
            remote(kv.at[0], kv.at[0], cs.at[d, k], cr.at[d, 0], twin).wait_send()
    for copy in pending:
        copy.wait_send()


def body(tokens, norm_gain, w_qkv, head_scale, w_out, scale_ids):
    rows, feat = tokens.shape
    dim = w_qkv.shape[1]
    dma = pltpu.SemaphoreType.DMA
    any_spec = pl.BlockSpec(memory_space=pl.ANY)
    vm = pl.BlockSpec(memory_space=pltpu.VMEM)
    return pl.pallas_call(
        kernel,
        name="branch",
        out_shape=jax.ShapeDtypeStruct((rows, feat), BF),
        in_specs=[any_spec, vm, any_spec, pl.BlockSpec(memory_space=pltpu.SMEM), any_spec, vm],
        out_specs=vm,
        scratch_shapes=[
            pltpu.VMEM((8, rows, feat), BF),
            pltpu.VMEM((3, dim, feat), BF),
            pltpu.VMEM((rows, 3 * feat), F32),
            pltpu.VMEM((rows, 128), F32),
            pltpu.VMEM((32, 2, 2, rows // 2, 128), BF),
            pltpu.VMEM((2, 2, rows // 2, 128), BF),
            pltpu.VMEM((2, rows, 128), BF),
            pltpu.VMEM((rows, 128), BF),
            pltpu.VMEM((2, rows, 128), F32),
            pltpu.VMEM((2, rows, 128), F32),
            pltpu.VMEM((2, rows, 128), F32),
            pltpu.VMEM((8, 2, 2, rows // 2, 128), BF),
            pltpu.VMEM((2, rows // 2, 128), BF),
            pltpu.VMEM((8, feat, feat), BF),
            dma((3,)),
            dma((1,)), dma((1,)), dma((8,)), dma((8,)),
            dma((2, 3)), dma((2, 3)), dma((2, 8)), dma((2, 8)),
            dma((8,)), dma((8,)),
            dma((3,)), dma((3,)),
            dma((2, 8)), dma((2, 8)),
            dma((3, 8)), dma((3, 8)),
        ],
        compiler_params=pltpu.CompilerParams(
            collective_id=0, has_side_effects=True, vmem_limit_bytes=56 * 1024 * 1024
        ),
        cost_estimate=pl.CostEstimate(flops=11_000_000_000, bytes_accessed=6_000_000, transcendentals=17_000_000),
    )(tokens, norm_gain.reshape(1, -1), w_qkv, head_scale.reshape(1, -1), w_out, scale_ids.reshape(-1, 128))


def solution(mesh):
    placed = (P("seq", "head"), P(), P(None, None, "head"), P("head"), P("head", None), P())
    return jax.shard_map(
        body, mesh=mesh, in_specs=placed, out_specs=P("seq", "head"), check_vma=False
    )
```

```python
import functools
import math

import jax
import jax.numpy as jnp
from jax import lax
from jax.experimental import pallas as pl
from jax.experimental.pallas import tpu as pltpu
from jax.sharding import PartitionSpec as P

MESH = pl.DeviceIdType.MESH
BF = jnp.bfloat16
F32 = jnp.float32
LOG2E = math.log2(math.e)


def kernel(
    tokens, gain, wqkv, hscale, wout, ids, out,
    xg, wq, acc3, ssq, kv, kvsend, qbuf, qsend, qid, oacc, lacc, attg, osend, wc,
    lsem, gs_x, gr_x, gs_y, gr_y, os, orr, ys, yr, ws, wr, xs, xr, zs, zr, cs, cr,
):
    rows, feat = tokens.shape
    hd_dim = 128
    sid = lax.axis_index("seq")
    hid = lax.axis_index("head")
    z, xl, c = sid // 4, (sid // 2) % 2, sid % 2
    xh, y = hid // 4, hid % 4

    def sq(zz, xx, cc):
        return lax.rem(zz + 8, 8) * 4 + xx * 2 + cc

    def hx(xx, yy):
        return xx * 4 + lax.rem(yy + 4, 4)

    def at_head(h):
        return (sid, h)

    def at_seq(s):
        return (s, hid)

    x_partner = at_head(hx(1 - xh, y))
    y_up, y_down = at_head(hx(xh, y + 1)), at_head(hx(xh, y - 1))
    pair = at_seq(sq(z, 1 - xl, c))
    twin = at_seq(sq(z, xl, 1 - c))
    diag = (sq(z, 1 - xl, c), hx(1 - xh, y))
    z_up, z_down = at_seq(sq(z + 1, xl, c)), at_seq(sq(z - 1, xl, c))

    def remote(src, dst, ssem, rsem, dev):
        return pltpu.make_async_remote_copy(
            src_ref=src, dst_ref=dst, send_sem=ssem, recv_sem=rsem, device_id=dev, device_id_type=MESH
        )

    own = pltpu.make_async_copy(tokens, xg.at[hid], lsem.at[0])
    own.start()
    loads = pltpu.make_async_copy(wqkv, wq, lsem.at[1])
    loads.start()
    own_w = pltpu.make_async_copy(wout.at[:, pl.ds(pl.multiple_of(hid * feat, feat), feat)], wc.at[hid], lsem.at[2])
    own_w.start()

    barrier = pltpu.get_barrier_semaphore()
    for d in range(1, 8):
        pl.semaphore_signal(barrier, inc=1, device_id=at_head(lax.rem(hid + d, 8)), device_id_type=MESH)
    for dev in (pair, twin, diag, z_up, z_down):
        pl.semaphore_signal(barrier, inc=1, device_id=dev, device_id_type=MESH)
    pl.semaphore_wait(barrier, 12)

    pending = []

    def go(copy):
        copy.start()
        pending.append(copy)
        return copy

    half = rows // 2
    mid = half // 2
    oid = hx(1 - xh, y)

    def part(ref, p, ch):
        return ref.at[p, pl.ds(ch * half, half)]

    for ch in range(2):
        mine = tokens.at[pl.ds(ch * half, half)]
        go(remote(mine, part(xg, hid, ch), gs_x.at[ch], gr_x.at[ch], x_partner))
        go(remote(mine, part(xg, hid, ch), gs_y.at[ch, 0], gr_y.at[ch, 0], y_up))
        go(remote(mine, part(xg, hid, ch), gs_y.at[ch, 1], gr_y.at[ch, 1], y_down))

    def piece_of(stage, i):
        if stage == 0:
            return lax.rem(xh + i, 2) * 4 + y
        if stage == 3:
            return lax.rem(xh + i, 2) * 4 + lax.rem(y + 2, 4)
        g = stage - 1
        return lax.rem(xh + g, 2) * 4 + lax.rem(y + 3 + 2 * i, 4)

    for i in range(2):
        for j in range(4):
            row = ids[pl.ds(sq(z, i, c) * 4 + j, 1), :]
            qid[i, pl.ds(j * 128, 128), :] = jnp.broadcast_to(row.astype(F32), (128, 128)).T
    oacc[...] = jnp.zeros_like(oacc)
    lacc[...] = jnp.zeros_like(lacc)
    acc3[...] = jnp.zeros_like(acc3)
    ssq[...] = jnp.zeros_like(ssq)

    def project(stage, ch):
        span = pl.ds(ch * half, half)

        def step(i, carry):
            p = piece_of(stage, i)
            lane = pl.ds(pl.multiple_of(p * feat, feat), feat)
            x = xg[p, span, :].astype(F32)
            sqv = x * x
            ssq[span, :] += sqv[:, :128] + sqv[:, 128:]
            xw = (x * gain[:, lane]).astype(BF)
            for j in range(3):
                acc3[span, j * feat:(j + 1) * feat] += jnp.dot(xw, wq[j, lane, :], preferred_element_type=F32)
            return carry

        lax.fori_loop(0, 2, step, 0)

    def pass_on(g, ch):
        xx = xh if g == 0 else 1 - xh
        lo, hi = hx(xx, y - 1), hx(xx, y + 1)
        top = xg.at[lo, pl.ds(ch * half, mid)]
        bottom = xg.at[hi, pl.ds(ch * half + mid, mid)]
        remote(part(xg, lo, ch), part(xg, lo, ch), gs_y.at[ch, 0], gr_y.at[ch, 2 * g], y_up).wait_recv()
        go(remote(top, top, gs_y.at[ch, 4 + 2 * g], gr_y.at[ch, 4 + 2 * g], y_up))
        remote(part(xg, hi, ch), part(xg, hi, ch), gs_y.at[ch, 1], gr_y.at[ch, 2 * g + 1], y_down).wait_recv()
        go(remote(bottom, bottom, gs_y.at[ch, 5 + 2 * g], gr_y.at[ch, 5 + 2 * g], y_down))

    def far_in(ch):
        for g, xx in ((0, xh), (1, 1 - xh)):
            far = hx(xx, y + 2)
            top = xg.at[far, pl.ds(ch * half, mid)]
            bottom = xg.at[far, pl.ds(ch * half + mid, mid)]
            remote(top, top, gs_y.at[ch, 4], gr_y.at[ch, 4 + 2 * g], y_up).wait_recv()
            remote(bottom, bottom, gs_y.at[ch, 5], gr_y.at[ch, 5 + 2 * g], y_down).wait_recv()

    for ch in range(2):
        pass_on(0, ch)
        slot = part(xg, oid, ch)
        remote(slot, slot, gs_x.at[ch], gr_x.at[ch], x_partner).wait_recv()
        go(remote(slot, slot, gs_y.at[ch, 2], gr_y.at[ch, 2], y_up))
        go(remote(slot, slot, gs_y.at[ch, 3], gr_y.at[ch, 3], y_down))
    own.wait()
    loads.wait()
    project(0, 0)
    project(1, 0)
    pass_on(1, 0)
    project(2, 0)
    project(0, 1)
    pass_on(1, 1)

    def unit(v, factor):
        power = jnp.sum(v * v, axis=-1, keepdims=True)
        return (v * lax.rsqrt(power + 1e-06) * factor).astype(BF)

    other = sq(z, 1 - xl, c)

    def ring_send(blk, ch, u):
        it = kv.at[blk, ch]
        go(remote(it, it, zs.at[0, ch, u], zr.at[0, ch, u], z_up))
        go(remote(it, it, zs.at[1, ch, u], zr.at[1, ch, u], z_down))
        go(remote(it, it, cs.at[2, ch, u], cr.at[2, ch, u], twin))

    def heads(ch):
        span = pl.ds(ch * half, half)
        r = lax.rsqrt(jnp.sum(ssq[span, :], axis=-1, keepdims=True) * (1.0 / (8 * feat)) + 1e-06)

        def head_of(j, h):
            return acc3[span, pl.ds(pl.multiple_of(j * feat + h * hd_dim, hd_dim), hd_dim)] * r

        kv[sid, ch, 0] = unit(head_of(1, xl), 1.0)
        kv[sid, ch, 1] = head_of(2, xl).astype(BF)
        ring_send(sid, ch, 0)
        kvsend[ch, 0] = unit(head_of(1, 1 - xl), 1.0)
        kvsend[ch, 1] = head_of(2, 1 - xl).astype(BF)
        go(remote(kvsend.at[ch], kv.at[sid, ch], xs.at[ch, 0], xr.at[ch, 0], pair))
        qsend[ch] = unit(head_of(0, 1 - xl), hscale[0, 1 - xl] * LOG2E)
        go(remote(qsend.at[ch], qbuf.at[xl, span], xs.at[ch, 1], xr.at[ch, 1], pair))
        qbuf[xl, span, :] = unit(head_of(0, xl), hscale[0, xl] * LOG2E)

    far_in(0)
    project(3, 0)
    heads(0)
    project(1, 1)
    project(2, 1)
    far_in(1)
    project(3, 1)
    heads(1)

    def block_at(dz, u, cc):
        return lax.rem(z + dz + 8, 8) * 4 + lax.rem(xl + u, 2) * 2 + cc

    def to_twin(blk, d, ch, k):
        return remote(kv.at[blk, ch], kv.at[blk, ch], cs.at[d, ch, k], cr.at[d, ch, k], twin)

    def from_twin(blk, d, k):
        for ch in range(2):
            remote(kv.at[blk, ch], kv.at[blk, ch], cs.at[d, ch, 0], cr.at[d, ch, k], twin).wait_recv()

    def landed(k, d, ch):
        s, u = k // 2 + 1, lax.rem(k, 2)
        blk = block_at(-s if d == 0 else s, u, c)
        remote(kv.at[blk, ch], kv.at[blk, ch], zs.at[d, ch, 0], zr.at[d, ch, k], z_up).wait_recv()
        return blk

    def events(k, ch, d):
        blk = landed(k, d, ch)
        it = kv.at[blk, ch]
        if d == 0:
            @pl.when(k <= 4)
            def _():
                remote(it, it, zs.at[0, ch, k + 2], zr.at[0, ch, k + 2], z_up).start()
        else:
            @pl.when(k <= 3)
            def _():
                remote(it, it, zs.at[1, ch, k + 2], zr.at[1, ch, k + 2], z_down).start()

            @pl.when(k == 5)
            def _():
                remote(it, it, zs.at[1, ch, k + 2], zr.at[1, ch, k + 2], z_down).start()
        to_twin(blk, d, ch, k).start()

    def pair_in(ch):
        remote(kvsend.at[ch], kv.at[other, ch], xs.at[ch, 0], xr.at[ch, 0], pair).wait_recv()
        ring_send(other, ch, 1)

    pair_in(0)
    events(0, 0, 0)
    events(0, 0, 1)
    pair_in(1)

    for d in range(1, 8):
        to = lax.rem(hid + d, 8)
        go(remote(
            wout.at[:, pl.ds(pl.multiple_of(to * feat, feat), feat)], wc.at[hid],
            ws.at[d], wr.at[d], at_head(to),
        ))
    events(0, 1, 0)
    events(0, 1, 1)
    for ch in range(2):
        slot = qbuf.at[1 - xl, pl.ds(ch * half, half)]
        remote(qsend.at[ch], slot, xs.at[ch, 1], xr.at[ch, 1], pair).wait_recv()

    def attend(blk, parts_of=(0, 1)):
        k = jnp.concatenate([kv[blk, 0, 0], kv[blk, 1, 0]], axis=0)
        v = jnp.concatenate([kv[blk, 0, 1], kv[blk, 1, 1]], axis=0)
        kids = [ids[pl.ds(blk * 4 + j, 1), :].astype(F32) for j in range(4)]
        for qh in parts_of:
            for i in range(2):
                span = pl.ds(qh * half, half)
                q = qbuf[i, span, :]
                s = lax.dot_general(q, k, (((1,), (1,)), ((), ())), preferred_element_type=F32)
                qi = qid[i, span, :]
                parts = []
                total = None
                for j in range(4):
                    e = jnp.where(kids[j] <= qi, jnp.exp2(s[:, j * 128:(j + 1) * 128]), 0.0)
                    total = e if total is None else total + e
                    parts.append(e.astype(BF))
                w = jnp.concatenate(parts, axis=1)
                oacc[i, span, :] += jnp.dot(w, v, preferred_element_type=F32)
                lacc[i, span, :] += total

    def loop2(f):
        lax.fori_loop(0, 2, lambda i, carry: (f(i), carry)[1], 0)

    loop2(lambda i: attend(block_at(0, i, c)))
    from_twin(block_at(0, 0, 1 - c), 2, 0)
    from_twin(block_at(0, 1, 1 - c), 2, 1)

    def period(p, carry):
        for ch in range(2):
            events(p, ch, 0)
            events(p, ch, 1)
        s, u = (p + 1) // 2, lax.rem(p - 1, 2)
        loop2(lambda i: attend(block_at((2 * i - 1) * s, u, c)))
        from_twin(block_at(-s, u, 1 - c), 0, p - 1)
        from_twin(block_at(s, u, 1 - c), 1, p - 1)
        loop2(lambda i: attend(block_at((2 * i - 1) * s, u, 1 - c)))
        return carry

    loop2(lambda i: attend(block_at(0, i, 1 - c)))
    lax.fori_loop(1, 6, period, 0)
    loop2(lambda i: attend(block_at((2 * i - 1) * 3, 1, c)))
    for ch in range(2):
        landed(6, 0, ch)
        go(to_twin(block_at(4, 0, c), 0, ch, 6))
        landed(7, 1, ch)
        go(to_twin(block_at(4, 1, c), 1, ch, 7))
    from_twin(block_at(-3, 1, 1 - c), 0, 5)
    from_twin(block_at(3, 1, 1 - c), 1, 5)
    loop2(lambda i: attend(block_at((2 * i - 1) * 3, 1, 1 - c)))
    def hand_out(qh):
        span = pl.ds(qh * half, half)

        def attended(i):
            total = jnp.sum(lacc[i, span, :], axis=-1, keepdims=True)
            return (oacc[i, span, :] / total).astype(BF)

        osend[qh] = attended(1 - xl)
        mine = attg.at[hid, qh, xl]
        go(remote(osend.at[qh], mine, os.at[qh, 0], orr.at[qh, 0], pair))
        go(remote(osend.at[qh], mine, os.at[qh, 1], orr.at[qh, 1], diag))
        attg[hid, qh, xl] = attended(xl)
        go(remote(mine, mine, os.at[qh, 2], orr.at[qh, 2], x_partner))

    loop2(lambda i: attend(block_at(4, i, c), (0,)))
    from_twin(block_at(4, 0, 1 - c), 0, 6)
    from_twin(block_at(4, 1, 1 - c), 1, 7)
    loop2(lambda i: attend(block_at(4, i, 1 - c), (0,)))
    hand_out(0)

    def last(i, carry):
        attend(lax.rem(z + 4, 8) * 4 + lax.rem(xl + i, 2) * 2 + lax.rem(c + i // 2, 2), (1,))
        return carry

    lax.fori_loop(0, 4, last, 0)
    hand_out(1)

    own_w.wait()
    for d in range(1, 8):
        frm = lax.rem(hid - d + 8, 8)
        remote(wc.at[frm], wc.at[frm], ws.at[d], wr.at[d], at_head(frm)).wait_recv()

    fin = acc3.at[:, pl.ds(0, feat)]
    fin[...] = jnp.zeros((rows, feat), F32)

    def finish(stage, qh):
        def step(i, carry):
            p = piece_of(stage, i)
            a = jnp.concatenate([attg[p, qh, 0], attg[p, qh, 1]], axis=1)
            fin[pl.ds(qh * half, half), :] += jnp.dot(a, wc[p], preferred_element_type=F32)
            return carry

        lax.fori_loop(0, 2, step, 0)

    for qh in range(2):
        slot = attg.at[hid, qh, 1 - xl]
        remote(slot, slot, os.at[qh, 0], orr.at[qh, 0], pair).wait_recv()
        whole = attg.at[hid, qh]
        go(remote(whole, whole, ys.at[qh, 0], yr.at[qh, 0], y_up))
        go(remote(whole, whole, ys.at[qh, 1], yr.at[qh, 1], y_down))
        slot = attg.at[oid, qh, 1 - xl]
        remote(slot, slot, os.at[qh, 1], orr.at[qh, 1], diag).wait_recv()
        slot = attg.at[oid, qh, xl]
        remote(slot, slot, os.at[qh, 2], orr.at[qh, 2], x_partner).wait_recv()
        whole = attg.at[oid, qh]
        go(remote(whole, whole, ys.at[qh, 2], yr.at[qh, 2], y_up))
        go(remote(whole, whole, ys.at[qh, 3], yr.at[qh, 3], y_down))
    finish(0, 0)
    finish(0, 1)
    for qh in range(2):
        for g, xx in ((0, xh), (1, 1 - xh)):
            lo, hi = attg.at[hx(xx, y - 1), qh], attg.at[hx(xx, y + 1), qh]
            remote(lo, lo, ys.at[qh, 0], yr.at[qh, 2 * g], y_up).wait_recv()
            go(remote(lo.at[0], lo.at[0], ys.at[qh, 4 + 2 * g], yr.at[qh, 4 + 2 * g], y_up))
            remote(hi, hi, ys.at[qh, 1], yr.at[qh, 2 * g + 1], y_down).wait_recv()
            go(remote(hi.at[1], hi.at[1], ys.at[qh, 5 + 2 * g], yr.at[qh, 5 + 2 * g], y_down))
            finish(1 + g, qh)
    for qh in range(2):
        for g, xx in ((0, xh), (1, 1 - xh)):
            far = attg.at[hx(xx, y + 2), qh]
            remote(far.at[0], far.at[0], ys.at[qh, 4], yr.at[qh, 4 + 2 * g], y_up).wait_recv()
            remote(far.at[1], far.at[1], ys.at[qh, 5], yr.at[qh, 5 + 2 * g], y_down).wait_recv()
        finish(3, qh)
    out[...] = fin[...].astype(BF)

    it = kv.at[0, 0]
    for ch in range(2):
        for k in range(2, 7):
            remote(it, it, zs.at[0, ch, k], zr.at[0, 0, 0], z_up).wait_send()
        for k in (2, 3, 4, 5, 7):
            remote(it, it, zs.at[1, ch, k], zr.at[1, 0, 0], z_down).wait_send()
        for k in range(6):
            for d in range(2):
                remote(it, it, cs.at[d, ch, k], cr.at[d, 0, 0], twin).wait_send()
    for copy in pending:
        copy.wait_send()


def body(tokens, norm_gain, w_qkv, head_scale, w_out, scale_ids):
    rows, feat = tokens.shape
    dim = w_qkv.shape[1]
    dma = pltpu.SemaphoreType.DMA
    any_spec = pl.BlockSpec(memory_space=pl.ANY)
    vm = pl.BlockSpec(memory_space=pltpu.VMEM)
    return pl.pallas_call(
        kernel,
        name="branch",
        out_shape=jax.ShapeDtypeStruct((rows, feat), BF),
        in_specs=[any_spec, vm, any_spec, pl.BlockSpec(memory_space=pltpu.SMEM), any_spec, vm],
        out_specs=vm,
        scratch_shapes=[
            pltpu.VMEM((8, rows, feat), BF),
            pltpu.VMEM((3, dim, feat), BF),
            pltpu.VMEM((rows, 3 * feat), F32),
            pltpu.VMEM((rows, 128), F32),
            pltpu.VMEM((32, 2, 2, rows // 2, 128), BF),
            pltpu.VMEM((2, 2, rows // 2, 128), BF),
            pltpu.VMEM((2, rows, 128), BF),
            pltpu.VMEM((2, rows // 2, 128), BF),
            pltpu.VMEM((2, rows, 128), F32),
            pltpu.VMEM((2, rows, 128), F32),
            pltpu.VMEM((2, rows, 128), F32),
            pltpu.VMEM((8, 2, 2, rows // 2, 128), BF),
            pltpu.VMEM((2, rows // 2, 128), BF),
            pltpu.VMEM((8, feat, feat), BF),
            dma((3,)),
            dma((2,)), dma((2,)), dma((2, 8)), dma((2, 8)),
            dma((2, 3)), dma((2, 3)), dma((2, 8)), dma((2, 8)),
            dma((8,)), dma((8,)),
            dma((2, 2)), dma((2, 2)),
            dma((2, 2, 8)), dma((2, 2, 8)),
            dma((3, 2, 8)), dma((3, 2, 8)),
        ],
        compiler_params=pltpu.CompilerParams(
            collective_id=0, has_side_effects=True, vmem_limit_bytes=56 * 1024 * 1024
        ),
        cost_estimate=pl.CostEstimate(flops=11_000_000_000, bytes_accessed=6_000_000, transcendentals=17_000_000),
    )(tokens, norm_gain.reshape(1, -1), w_qkv, head_scale.reshape(1, -1), w_out, scale_ids.reshape(-1, 128))


def solution(mesh):
    placed = (P("seq", "head"), P(), P(None, None, "head"), P("head"), P("head", None), P())
    return jax.shard_map(
        body, mesh=mesh, in_specs=placed, out_specs=P("seq", "head"), check_vma=False
    )
```

```python
import functools
import math

import jax
import jax.numpy as jnp
from jax import lax
from jax.experimental import pallas as pl
from jax.experimental.pallas import tpu as pltpu
from jax.sharding import PartitionSpec as P

MESH = pl.DeviceIdType.MESH
BF = jnp.bfloat16
F32 = jnp.float32
LOG2E = math.log2(math.e)


def kernel(
    tokens, gain, wqkv, hscale, wout, ids, out,
    xg, wq, acc3, ssq, kv, kvsend, qbuf, qsend, qid, oacc, lacc, attg, osend, wc,
    lsem, gs_x, gr_x, gs_y, gr_y, os, orr, ys, yr, ws, wr, xs, xr, zs, zr, cs, cr,
):
    rows, feat = tokens.shape
    hd_dim = 128
    sid = lax.axis_index("seq")
    hid = lax.axis_index("head")
    z, xl, c = sid // 4, (sid // 2) % 2, sid % 2
    xh, y = hid // 4, hid % 4

    def sq(zz, xx, cc):
        return lax.rem(zz + 8, 8) * 4 + xx * 2 + cc

    def hx(xx, yy):
        return xx * 4 + lax.rem(yy + 4, 4)

    def at_head(h):
        return (sid, h)

    def at_seq(s):
        return (s, hid)

    x_partner = at_head(hx(1 - xh, y))
    y_up, y_down = at_head(hx(xh, y + 1)), at_head(hx(xh, y - 1))
    pair = at_seq(sq(z, 1 - xl, c))
    twin = at_seq(sq(z, xl, 1 - c))
    diag = (sq(z, 1 - xl, c), hx(1 - xh, y))
    z_up, z_down = at_seq(sq(z + 1, xl, c)), at_seq(sq(z - 1, xl, c))

    def remote(src, dst, ssem, rsem, dev):
        return pltpu.make_async_remote_copy(
            src_ref=src, dst_ref=dst, send_sem=ssem, recv_sem=rsem, device_id=dev, device_id_type=MESH
        )

    own = pltpu.make_async_copy(tokens, xg.at[hid], lsem.at[0])
    own.start()
    loads = pltpu.make_async_copy(wqkv, wq, lsem.at[1])
    loads.start()
    own_w = pltpu.make_async_copy(wout.at[:, pl.ds(pl.multiple_of(hid * feat, feat), feat)], wc.at[hid], lsem.at[2])
    own_w.start()

    barrier = pltpu.get_barrier_semaphore()
    for d in range(1, 8):
        pl.semaphore_signal(barrier, inc=1, device_id=at_head(lax.rem(hid + d, 8)), device_id_type=MESH)
    for dev in (pair, twin, diag, z_up, z_down):
        pl.semaphore_signal(barrier, inc=1, device_id=dev, device_id_type=MESH)
    pl.semaphore_wait(barrier, 12)

    pending = []

    def go(copy):
        copy.start()
        pending.append(copy)
        return copy

    half = rows // 2
    mid = half // 2
    oid = hx(1 - xh, y)

    def part(ref, p, ch):
        return ref.at[p, pl.ds(ch * half, half)]

    for ch in range(2):
        mine = tokens.at[pl.ds(ch * half, half)]
        go(remote(mine, part(xg, hid, ch), gs_x.at[ch, 0], gr_x.at[ch, 0], x_partner))
        go(remote(mine, part(xg, hid, ch), gs_y.at[ch, 0], gr_y.at[ch, 0], y_up))
        go(remote(mine, part(xg, hid, ch), gs_y.at[ch, 1], gr_y.at[ch, 1], y_down))

    def piece_of(stage, i):
        if stage == 0:
            return lax.rem(xh + i, 2) * 4 + y
        if stage == 3:
            return lax.rem(xh + i, 2) * 4 + lax.rem(y + 2, 4)
        g = stage - 1
        return lax.rem(xh + g, 2) * 4 + lax.rem(y + 3 + 2 * i, 4)

    for i in range(2):
        for j in range(4):
            row = ids[pl.ds(sq(z, i, c) * 4 + j, 1), :]
            qid[i, pl.ds(j * 128, 128), :] = jnp.broadcast_to(row.astype(F32), (128, 128)).T
    oacc[...] = jnp.zeros_like(oacc)
    lacc[...] = jnp.zeros_like(lacc)
    acc3[...] = jnp.zeros_like(acc3)
    ssq[...] = jnp.zeros_like(ssq)

    def project(stage, ch):
        span = pl.ds(ch * half, half)

        def step(i, carry):
            p = piece_of(stage, i)
            lane = pl.ds(pl.multiple_of(p * feat, feat), feat)
            x = xg[p, span, :].astype(F32)
            sqv = x * x
            ssq[span, :] += sqv[:, :128] + sqv[:, 128:]
            xw = (x * gain[:, lane]).astype(BF)
            for j in range(3):
                acc3[span, j * feat:(j + 1) * feat] += jnp.dot(xw, wq[j, lane, :], preferred_element_type=F32)
            return carry

        lax.fori_loop(0, 2, step, 0)

    def pass_on(g, ch):
        xx = xh if g == 0 else 1 - xh
        lo, hi = hx(xx, y - 1), hx(xx, y + 1)
        top = xg.at[lo, pl.ds(ch * half, mid)]
        bottom = xg.at[hi, pl.ds(ch * half + mid, mid)]
        remote(part(xg, lo, ch), part(xg, lo, ch), gs_y.at[ch, 0], gr_y.at[ch, 2 * g], y_up).wait_recv()
        go(remote(top, top, gs_y.at[ch, 4 + 2 * g], gr_y.at[ch, 4 + 2 * g], y_up))
        remote(part(xg, hi, ch), part(xg, hi, ch), gs_y.at[ch, 1], gr_y.at[ch, 2 * g + 1], y_down).wait_recv()
        go(remote(bottom, bottom, gs_y.at[ch, 5 + 2 * g], gr_y.at[ch, 5 + 2 * g], y_down))

    def far_in(ch, *which):
        for g in which:
            far = hx(xh if g == 0 else 1 - xh, y + 2)
            top = xg.at[far, pl.ds(ch * half, mid)]
            bottom = xg.at[far, pl.ds(ch * half + mid, mid)]
            remote(top, top, gs_y.at[ch, 4], gr_y.at[ch, 4 + 2 * g], y_up).wait_recv()
            remote(bottom, bottom, gs_y.at[ch, 5], gr_y.at[ch, 5 + 2 * g], y_down).wait_recv()

    def swap_in(p, ch, k):
        slot = part(xg, p, ch)
        remote(slot, slot, gs_x.at[ch, 0], gr_x.at[ch, k], x_partner).wait_recv()
        return slot

    def swap_out(p, ch, k):
        slot = part(xg, p, ch)
        go(remote(slot, slot, gs_x.at[ch, k], gr_x.at[ch, k], x_partner))

    pass_on(0, 0)
    slot = swap_in(oid, 0, 0)
    go(remote(slot, slot, gs_y.at[0, 2], gr_y.at[0, 2], y_up))
    go(remote(slot, slot, gs_y.at[0, 3], gr_y.at[0, 3], y_down))
    pass_on(0, 1)
    swap_out(hx(xh, y - 1), 1, 1)
    swap_out(hx(xh, y + 1), 1, 2)
    own.wait()
    loads.wait()
    project(0, 0)
    project(1, 0)
    pass_on(1, 0)
    project(2, 0)
    project(1, 1)
    far_in(1, 0)
    swap_out(hx(xh, y + 2), 1, 3)

    def unit(v, factor):
        power = jnp.sum(v * v, axis=-1, keepdims=True)
        return (v * lax.rsqrt(power + 1e-06) * factor).astype(BF)

    other = sq(z, 1 - xl, c)

    def ring_send(blk, ch, u):
        it = kv.at[blk, ch]
        go(remote(it, it, zs.at[0, ch, u], zr.at[0, ch, u], z_up))
        go(remote(it, it, zs.at[1, ch, u], zr.at[1, ch, u], z_down))
        go(remote(it, it, cs.at[2, ch, u], cr.at[2, ch, u], twin))

    def heads(ch):
        span = pl.ds(ch * half, half)
        r = lax.rsqrt(jnp.sum(ssq[span, :], axis=-1, keepdims=True) * (1.0 / (8 * feat)) + 1e-06)

        def head_of(j, h):
            return acc3[span, pl.ds(pl.multiple_of(j * feat + h * hd_dim, hd_dim), hd_dim)] * r

        kv[sid, ch, 0] = unit(head_of(1, xl), 1.0)
        kv[sid, ch, 1] = head_of(2, xl).astype(BF)
        ring_send(sid, ch, 0)
        kvsend[ch, 0] = unit(head_of(1, 1 - xl), 1.0)
        kvsend[ch, 1] = head_of(2, 1 - xl).astype(BF)
        go(remote(kvsend.at[ch], kv.at[sid, ch], xs.at[ch, 0], xr.at[ch, 0], pair))
        qsend[ch] = unit(head_of(0, 1 - xl), hscale[0, 1 - xl] * LOG2E)
        go(remote(qsend.at[ch], qbuf.at[xl, span], xs.at[ch, 1], xr.at[ch, 1], pair))
        qbuf[xl, span, :] = unit(head_of(0, xl), hscale[0, xl] * LOG2E)

    far_in(0, 0, 1)
    project(3, 0)
    heads(0)
    swap_in(oid, 1, 0)
    project(0, 1)
    swap_in(hx(1 - xh, y - 1), 1, 1)
    swap_in(hx(1 - xh, y + 1), 1, 2)
    project(2, 1)
    swap_in(hx(1 - xh, y + 2), 1, 3)
    project(3, 1)
    heads(1)

    def block_at(dz, u, cc):
        return lax.rem(z + dz + 8, 8) * 4 + lax.rem(xl + u, 2) * 2 + cc

    def to_twin(blk, d, ch, k):
        return remote(kv.at[blk, ch], kv.at[blk, ch], cs.at[d, ch, k], cr.at[d, ch, k], twin)

    def from_twin(blk, d, k):
        for ch in range(2):
            remote(kv.at[blk, ch], kv.at[blk, ch], cs.at[d, ch, 0], cr.at[d, ch, k], twin).wait_recv()

    def landed(k, d, ch):
        s, u = k // 2 + 1, lax.rem(k, 2)
        blk = block_at(-s if d == 0 else s, u, c)
        remote(kv.at[blk, ch], kv.at[blk, ch], zs.at[d, ch, 0], zr.at[d, ch, k], z_up).wait_recv()
        return blk

    def events(k, ch, d):
        blk = landed(k, d, ch)
        it = kv.at[blk, ch]
        if d == 0:
            @pl.when(k <= 4)
            def _():
                remote(it, it, zs.at[0, ch, k + 2], zr.at[0, ch, k + 2], z_up).start()
        else:
            @pl.when(k <= 3)
            def _():
                remote(it, it, zs.at[1, ch, k + 2], zr.at[1, ch, k + 2], z_down).start()

            @pl.when(k == 5)
            def _():
                remote(it, it, zs.at[1, ch, k + 2], zr.at[1, ch, k + 2], z_down).start()
        to_twin(blk, d, ch, k).start()

    def pair_in(ch):
        remote(kvsend.at[ch], kv.at[other, ch], xs.at[ch, 0], xr.at[ch, 0], pair).wait_recv()
        ring_send(other, ch, 1)

    pair_in(0)
    events(0, 0, 0)
    events(0, 0, 1)
    pair_in(1)

    for d in range(1, 8):
        to = lax.rem(hid + d, 8)
        go(remote(
            wout.at[:, pl.ds(pl.multiple_of(to * feat, feat), feat)], wc.at[hid],
            ws.at[d], wr.at[d], at_head(to),
        ))
    events(0, 1, 0)
    events(0, 1, 1)
    for ch in range(2):
        slot = qbuf.at[1 - xl, pl.ds(ch * half, half)]
        remote(qsend.at[ch], slot, xs.at[ch, 1], xr.at[ch, 1], pair).wait_recv()

    def attend(blk, parts_of=(0, 1)):
        k = jnp.concatenate([kv[blk, 0, 0], kv[blk, 1, 0]], axis=0)
        v = jnp.concatenate([kv[blk, 0, 1], kv[blk, 1, 1]], axis=0)
        kids = [ids[pl.ds(blk * 4 + j, 1), :].astype(F32) for j in range(4)]
        for qh in parts_of:
            for i in range(2):
                span = pl.ds(qh * half, half)
                q = qbuf[i, span, :]
                s = lax.dot_general(q, k, (((1,), (1,)), ((), ())), preferred_element_type=F32)
                qi = qid[i, span, :]
                parts = []
                total = None
                for j in range(4):
                    e = jnp.where(kids[j] <= qi, jnp.exp2(s[:, j * 128:(j + 1) * 128]), 0.0)
                    total = e if total is None else total + e
                    parts.append(e.astype(BF))
                w = jnp.concatenate(parts, axis=1)
                oacc[i, span, :] += jnp.dot(w, v, preferred_element_type=F32)
                lacc[i, span, :] += total

    def loop2(f):
        lax.fori_loop(0, 2, lambda i, carry: (f(i), carry)[1], 0)

    loop2(lambda i: attend(block_at(0, i, c)))
    from_twin(block_at(0, 0, 1 - c), 2, 0)
    from_twin(block_at(0, 1, 1 - c), 2, 1)

    def period(p, carry):
        for ch in range(2):
            events(p, ch, 0)
            events(p, ch, 1)
        s, u = (p + 1) // 2, lax.rem(p - 1, 2)
        loop2(lambda i: attend(block_at((2 * i - 1) * s, u, c)))
        from_twin(block_at(-s, u, 1 - c), 0, p - 1)
        from_twin(block_at(s, u, 1 - c), 1, p - 1)
        loop2(lambda i: attend(block_at((2 * i - 1) * s, u, 1 - c)))
        return carry

    loop2(lambda i: attend(block_at(0, i, 1 - c)))
    lax.fori_loop(1, 6, period, 0)
    loop2(lambda i: attend(block_at((2 * i - 1) * 3, 1, c)))
    for ch in range(2):
        landed(6, 0, ch)
        go(to_twin(block_at(4, 0, c), 0, ch, 6))
        landed(7, 1, ch)
        go(to_twin(block_at(4, 1, c), 1, ch, 7))
    from_twin(block_at(-3, 1, 1 - c), 0, 5)
    from_twin(block_at(3, 1, 1 - c), 1, 5)
    loop2(lambda i: attend(block_at((2 * i - 1) * 3, 1, 1 - c)))
    def attended(i, qh):
        span = pl.ds(qh * half, half)
        total = jnp.sum(lacc[i, span, :], axis=-1, keepdims=True)
        return (oacc[i, span, :] / total).astype(BF)

    def over_x(qh, step, yy, theirs):
        mine = attg.at[hx(xh, yy), qh, xl]
        go(remote(theirs, mine, os.at[qh, step, 0], orr.at[qh, step, 0], pair))
        go(remote(theirs, mine, os.at[qh, step, 1], orr.at[qh, step, 1], diag))
        go(remote(mine, mine, os.at[qh, step, 2], orr.at[qh, step, 2], x_partner))

    def from_x(qh, step, yy):
        for k, (xx, hh, dev) in enumerate(((xh, 1 - xl, pair), (1 - xh, 1 - xl, diag), (1 - xh, xl, x_partner))):
            slot = attg.at[hx(xx, yy), qh, hh]
            remote(slot, slot, os.at[qh, 0, k], orr.at[qh, step, k], dev).wait_recv()

    loop2(lambda i: attend(block_at(4, i, c), (0,)))
    from_twin(block_at(4, 0, 1 - c), 0, 6)
    from_twin(block_at(4, 1, 1 - c), 1, 7)
    loop2(lambda i: attend(block_at(4, i, 1 - c), (0,)))
    osend[y, 0] = attended(1 - xl, 0)
    attg[hid, 0, xl] = attended(xl, 0)
    over_x(0, 0, y, osend.at[y, 0])

    def last(i, carry):
        attend(lax.rem(z + 4, 8) * 4 + lax.rem(xl + i, 2) * 2 + lax.rem(c + i // 2, 2), (1,))
        return carry

    lax.fori_loop(0, 4, last, 0)
    osend[y, 1] = attended(1 - xl, 1)
    attg[hid, 1, xl] = attended(xl, 1)
    theirs, ours = osend.at[y, 1], attg.at[hid, 1, xl]
    for k, dev in enumerate((y_up, y_down)):
        go(remote(theirs, theirs, ys.at[1, k], yr.at[1, k], dev))
        go(remote(ours, ours, ys.at[1, 2 + k], yr.at[1, 2 + k], dev))
    over_x(1, 0, y, theirs)

    slot = attg.at[hid, 0, 1 - xl]
    remote(slot, slot, os.at[0, 0, 0], orr.at[0, 0, 0], pair).wait_recv()
    whole = attg.at[hid, 0]
    go(remote(whole, whole, ys.at[0, 0], yr.at[0, 0], y_up))
    go(remote(whole, whole, ys.at[0, 1], yr.at[0, 1], y_down))
    lo, hi = lax.rem(y + 3, 4), lax.rem(y + 1, 4)
    for k, yy in enumerate((lo, hi)):
        theirs, ours = osend.at[yy, 1], attg.at[hx(xh, yy), 1, xl]
        dev = (y_up, y_down)[k]
        remote(theirs, theirs, ys.at[1, 0], yr.at[1, k], dev).wait_recv()
        remote(ours, ours, ys.at[1, 0], yr.at[1, 2 + k], dev).wait_recv()
        it = (theirs, ours)[k]
        go(remote(it, it, ys.at[1, 4 + k], yr.at[1, 4 + k], dev))
        over_x(1, 1 + k, yy, theirs)
    slot = attg.at[oid, 0, 1 - xl]
    remote(slot, slot, os.at[0, 0, 1], orr.at[0, 0, 1], diag).wait_recv()
    slot = attg.at[oid, 0, xl]
    remote(slot, slot, os.at[0, 0, 2], orr.at[0, 0, 2], x_partner).wait_recv()
    whole = attg.at[oid, 0]
    go(remote(whole, whole, ys.at[0, 2], yr.at[0, 2], y_up))
    go(remote(whole, whole, ys.at[0, 3], yr.at[0, 3], y_down))

    own_w.wait()
    for d in range(1, 8):
        frm = lax.rem(hid - d + 8, 8)
        remote(wc.at[frm], wc.at[frm], ws.at[d], wr.at[d], at_head(frm)).wait_recv()

    fin = acc3.at[:, pl.ds(0, feat)]
    fin[...] = jnp.zeros((rows, feat), F32)

    def finish(stage, qh):
        def step(i, carry):
            p = piece_of(stage, i)
            a = jnp.concatenate([attg[p, qh, 0], attg[p, qh, 1]], axis=1)
            fin[pl.ds(qh * half, half), :] += jnp.dot(a, wc[p], preferred_element_type=F32)
            return carry

        lax.fori_loop(0, 2, step, 0)

    finish(0, 0)

    def pass_half(g):
        xx = xh if g == 0 else 1 - xh
        lo, hi = attg.at[hx(xx, y - 1), 0], attg.at[hx(xx, y + 1), 0]
        remote(lo, lo, ys.at[0, 0], yr.at[0, 2 * g], y_up).wait_recv()
        go(remote(lo.at[0], lo.at[0], ys.at[0, 4 + 2 * g], yr.at[0, 4 + 2 * g], y_up))
        remote(hi, hi, ys.at[0, 1], yr.at[0, 2 * g + 1], y_down).wait_recv()
        go(remote(hi.at[1], hi.at[1], ys.at[0, 5 + 2 * g], yr.at[0, 5 + 2 * g], y_down))
        finish(1 + g, 0)

    pass_half(0)
    far = lax.rem(y + 2, 4)
    theirs, ours = osend.at[far, 1], attg.at[hx(xh, far), 1, xl]
    remote(theirs, theirs, ys.at[1, 0], yr.at[1, 4], y_up).wait_recv()
    remote(ours, ours, ys.at[1, 0], yr.at[1, 5], y_down).wait_recv()
    over_x(1, 3, far, theirs)
    pass_half(1)
    from_x(1, 0, y)
    finish(0, 1)
    from_x(1, 1, lo)
    from_x(1, 2, hi)
    finish(1, 1)
    finish(2, 1)
    for g, xx in ((0, xh), (1, 1 - xh)):
        piece = attg.at[hx(xx, y + 2), 0]
        remote(piece.at[0], piece.at[0], ys.at[0, 4], yr.at[0, 4 + 2 * g], y_up).wait_recv()
        remote(piece.at[1], piece.at[1], ys.at[0, 5], yr.at[0, 5 + 2 * g], y_down).wait_recv()
    finish(3, 0)
    from_x(1, 3, far)
    finish(3, 1)
    out[...] = fin[...].astype(BF)

    it = kv.at[0, 0]
    for ch in range(2):
        for k in range(2, 7):
            remote(it, it, zs.at[0, ch, k], zr.at[0, 0, 0], z_up).wait_send()
        for k in (2, 3, 4, 5, 7):
            remote(it, it, zs.at[1, ch, k], zr.at[1, 0, 0], z_down).wait_send()
        for k in range(6):
            for d in range(2):
                remote(it, it, cs.at[d, ch, k], cr.at[d, 0, 0], twin).wait_send()
    for copy in pending:
        copy.wait_send()


def body(tokens, norm_gain, w_qkv, head_scale, w_out, scale_ids):
    rows, feat = tokens.shape
    dim = w_qkv.shape[1]
    dma = pltpu.SemaphoreType.DMA
    any_spec = pl.BlockSpec(memory_space=pl.ANY)
    vm = pl.BlockSpec(memory_space=pltpu.VMEM)
    return pl.pallas_call(
        kernel,
        name="branch",
        out_shape=jax.ShapeDtypeStruct((rows, feat), BF),
        in_specs=[any_spec, vm, any_spec, pl.BlockSpec(memory_space=pltpu.SMEM), any_spec, vm],
        out_specs=vm,
        scratch_shapes=[
            pltpu.VMEM((8, rows, feat), BF),
            pltpu.VMEM((3, dim, feat), BF),
            pltpu.VMEM((rows, 3 * feat), F32),
            pltpu.VMEM((rows, 128), F32),
            pltpu.VMEM((32, 2, 2, rows // 2, 128), BF),
            pltpu.VMEM((2, 2, rows // 2, 128), BF),
            pltpu.VMEM((2, rows, 128), BF),
            pltpu.VMEM((2, rows // 2, 128), BF),
            pltpu.VMEM((2, rows, 128), F32),
            pltpu.VMEM((2, rows, 128), F32),
            pltpu.VMEM((2, rows, 128), F32),
            pltpu.VMEM((8, 2, 2, rows // 2, 128), BF),
            pltpu.VMEM((4, 2, rows // 2, 128), BF),
            pltpu.VMEM((8, feat, feat), BF),
            dma((3,)),
            dma((2, 4)), dma((2, 4)), dma((2, 8)), dma((2, 8)),
            dma((2, 4, 3)), dma((2, 4, 3)), dma((2, 8)), dma((2, 8)),
            dma((8,)), dma((8,)),
            dma((2, 2)), dma((2, 2)),
            dma((2, 2, 8)), dma((2, 2, 8)),
            dma((3, 2, 8)), dma((3, 2, 8)),
        ],
        compiler_params=pltpu.CompilerParams(
            collective_id=0, has_side_effects=True, vmem_limit_bytes=56 * 1024 * 1024
        ),
        cost_estimate=pl.CostEstimate(flops=11_000_000_000, bytes_accessed=6_000_000, transcendentals=17_000_000),
    )(tokens, norm_gain.reshape(1, -1), w_qkv, head_scale.reshape(1, -1), w_out, scale_ids.reshape(-1, 128))


def solution(mesh):
    placed = (P("seq", "head"), P(), P(None, None, "head"), P("head"), P("head", None), P())
    return jax.shard_map(
        body, mesh=mesh, in_specs=placed, out_specs=P("seq", "head"), check_vma=False
    )
```

```python
import functools
import math

import jax
import jax.numpy as jnp
from jax import lax
from jax.experimental import pallas as pl
from jax.experimental.pallas import tpu as pltpu
from jax.sharding import PartitionSpec as P

MESH = pl.DeviceIdType.MESH
BF = jnp.bfloat16
F32 = jnp.float32
LOG2E = math.log2(math.e)


def kernel(
    tokens, gain, wqkv, hscale, wout, ids, out,
    xg, wq, acc3, ssq, kv, kvsend, qbuf, qsend, qid, oacc, lacc, attg, osend, wc,
    lsem, gs_x, gr_x, gs_y, gr_y, os, orr, ys, yr, ws, wr, xs, xr, zs, zr, cs, cr,
):
    rows, feat = tokens.shape
    hd_dim = 128
    sid = lax.axis_index("seq")
    hid = lax.axis_index("head")
    z, xl, c = sid // 4, (sid // 2) % 2, sid % 2
    xh, y = hid // 4, hid % 4

    def sq(zz, xx, cc):
        return lax.rem(zz + 8, 8) * 4 + xx * 2 + cc

    def hx(xx, yy):
        return xx * 4 + lax.rem(yy + 4, 4)

    def at_head(h):
        return (sid, h)

    def at_seq(s):
        return (s, hid)

    x_partner = at_head(hx(1 - xh, y))
    y_up, y_down = at_head(hx(xh, y + 1)), at_head(hx(xh, y - 1))
    pair = at_seq(sq(z, 1 - xl, c))
    twin = at_seq(sq(z, xl, 1 - c))
    diag = (sq(z, 1 - xl, c), hx(1 - xh, y))
    z_up, z_down = at_seq(sq(z + 1, xl, c)), at_seq(sq(z - 1, xl, c))

    def remote(src, dst, ssem, rsem, dev):
        return pltpu.make_async_remote_copy(
            src_ref=src, dst_ref=dst, send_sem=ssem, recv_sem=rsem, device_id=dev, device_id_type=MESH
        )

    own = pltpu.make_async_copy(tokens, xg.at[hid], lsem.at[0])
    own.start()
    loads = pltpu.make_async_copy(wqkv, wq, lsem.at[1])
    loads.start()
    own_w = pltpu.make_async_copy(wout.at[:, pl.ds(pl.multiple_of(hid * feat, feat), feat)], wc.at[hid], lsem.at[2])
    own_w.start()

    barrier = pltpu.get_barrier_semaphore()
    for d in range(1, 8):
        pl.semaphore_signal(barrier, inc=1, device_id=at_head(lax.rem(hid + d, 8)), device_id_type=MESH)
    for dev in (pair, twin, diag, z_up, z_down):
        pl.semaphore_signal(barrier, inc=1, device_id=dev, device_id_type=MESH)
    pl.semaphore_wait(barrier, 12)

    pending = []

    def go(copy):
        copy.start()
        pending.append(copy)
        return copy

    half = rows // 2
    mid = half // 2
    oid = hx(1 - xh, y)

    def part(ref, p, ch):
        return ref.at[p, pl.ds(ch * half, half)]

    for ch in range(2):
        mine = tokens.at[pl.ds(ch * half, half)]
        go(remote(mine, part(xg, hid, ch), gs_x.at[ch, 0], gr_x.at[ch, 0], x_partner))
        go(remote(mine, part(xg, hid, ch), gs_y.at[ch, 0], gr_y.at[ch, 0], y_up))
        go(remote(mine, part(xg, hid, ch), gs_y.at[ch, 1], gr_y.at[ch, 1], y_down))

    def piece_of(stage, i):
        if stage == 0:
            return lax.rem(xh + i, 2) * 4 + y
        if stage == 3:
            return lax.rem(xh + i, 2) * 4 + lax.rem(y + 2, 4)
        g = stage - 1
        return lax.rem(xh + g, 2) * 4 + lax.rem(y + 3 + 2 * i, 4)

    for i in range(2):
        for j in range(4):
            row = ids[pl.ds(sq(z, i, c) * 4 + j, 1), :]
            qid[i, pl.ds(j * 128, 128), :] = jnp.broadcast_to(row.astype(F32), (128, 128)).T
    oacc[...] = jnp.zeros_like(oacc)
    lacc[...] = jnp.zeros_like(lacc)
    acc3[...] = jnp.zeros_like(acc3)
    ssq[...] = jnp.zeros_like(ssq)

    def project(stage, ch):
        span = pl.ds(ch * half, half)

        def step(i, carry):
            p = piece_of(stage, i)
            lane = pl.ds(pl.multiple_of(p * feat, feat), feat)
            x = xg[p, span, :].astype(F32)
            sqv = x * x
            ssq[span, :] += sqv[:, :128] + sqv[:, 128:]
            xw = (x * gain[:, lane]).astype(BF)
            for j in range(3):
                acc3[span, j * feat:(j + 1) * feat] += jnp.dot(xw, wq[j, lane, :], preferred_element_type=F32)
            return carry

        lax.fori_loop(0, 2, step, 0)

    def pass_on(g, ch):
        xx = xh if g == 0 else 1 - xh
        lo, hi = hx(xx, y - 1), hx(xx, y + 1)
        top = xg.at[lo, pl.ds(ch * half, mid)]
        bottom = xg.at[hi, pl.ds(ch * half + mid, mid)]
        remote(part(xg, lo, ch), part(xg, lo, ch), gs_y.at[ch, 0], gr_y.at[ch, 2 * g], y_up).wait_recv()
        go(remote(top, top, gs_y.at[ch, 4 + 2 * g], gr_y.at[ch, 4 + 2 * g], y_up))
        remote(part(xg, hi, ch), part(xg, hi, ch), gs_y.at[ch, 1], gr_y.at[ch, 2 * g + 1], y_down).wait_recv()
        go(remote(bottom, bottom, gs_y.at[ch, 5 + 2 * g], gr_y.at[ch, 5 + 2 * g], y_down))

    def far_in(ch, *which):
        for g in which:
            far = hx(xh if g == 0 else 1 - xh, y + 2)
            top = xg.at[far, pl.ds(ch * half, mid)]
            bottom = xg.at[far, pl.ds(ch * half + mid, mid)]
            remote(top, top, gs_y.at[ch, 4], gr_y.at[ch, 4 + 2 * g], y_up).wait_recv()
            remote(bottom, bottom, gs_y.at[ch, 5], gr_y.at[ch, 5 + 2 * g], y_down).wait_recv()

    def swap_in(p, ch, k):
        slot = part(xg, p, ch)
        remote(slot, slot, gs_x.at[ch, 0], gr_x.at[ch, k], x_partner).wait_recv()
        return slot

    def swap_out(p, ch, k):
        slot = part(xg, p, ch)
        go(remote(slot, slot, gs_x.at[ch, k], gr_x.at[ch, k], x_partner))

    pass_on(0, 0)
    slot = swap_in(oid, 0, 0)
    go(remote(slot, slot, gs_y.at[0, 2], gr_y.at[0, 2], y_up))
    go(remote(slot, slot, gs_y.at[0, 3], gr_y.at[0, 3], y_down))
    pass_on(0, 1)
    swap_out(hx(xh, y - 1), 1, 1)
    swap_out(hx(xh, y + 1), 1, 2)
    own.wait()
    loads.wait()
    project(0, 0)
    project(1, 0)
    pass_on(1, 0)
    project(2, 0)
    project(1, 1)
    far_in(1, 0)
    swap_out(hx(xh, y + 2), 1, 3)

    def unit(v, factor):
        power = jnp.sum(v * v, axis=-1, keepdims=True)
        return (v * lax.rsqrt(power + 1e-06) * factor).astype(BF)

    other = sq(z, 1 - xl, c)

    def ring_send(blk, ch, u):
        it = kv.at[blk, ch]
        go(remote(it, it, zs.at[0, ch, u], zr.at[0, ch, u], z_up))
        go(remote(it, it, zs.at[1, ch, u], zr.at[1, ch, u], z_down))
        go(remote(it, it, cs.at[2, ch, u], cr.at[2, ch, u], twin))

    def heads(ch):
        span = pl.ds(ch * half, half)
        r = lax.rsqrt(jnp.sum(ssq[span, :], axis=-1, keepdims=True) * (1.0 / (8 * feat)) + 1e-06)

        def head_of(j, h):
            return acc3[span, pl.ds(pl.multiple_of(j * feat + h * hd_dim, hd_dim), hd_dim)] * r

        kv[sid, ch, 0] = unit(head_of(1, xl), 1.0)
        kv[sid, ch, 1] = head_of(2, xl).astype(BF)
        ring_send(sid, ch, 0)
        kvsend[ch, 0] = unit(head_of(1, 1 - xl), 1.0)
        kvsend[ch, 1] = head_of(2, 1 - xl).astype(BF)
        go(remote(kvsend.at[ch], kv.at[sid, ch], xs.at[ch, 0], xr.at[ch, 0], pair))
        qsend[ch] = unit(head_of(0, 1 - xl), hscale[0, 1 - xl] * LOG2E)
        go(remote(qsend.at[ch], qbuf.at[xl, span], xs.at[ch, 1], xr.at[ch, 1], pair))
        qbuf[xl, span, :] = unit(head_of(0, xl), hscale[0, xl] * LOG2E)

    far_in(0, 0, 1)
    project(3, 0)
    heads(0)
    swap_in(oid, 1, 0)
    project(0, 1)
    swap_in(hx(1 - xh, y - 1), 1, 1)
    swap_in(hx(1 - xh, y + 1), 1, 2)
    project(2, 1)
    swap_in(hx(1 - xh, y + 2), 1, 3)
    project(3, 1)
    heads(1)

    def block_at(dz, u, cc):
        return lax.rem(z + dz + 8, 8) * 4 + lax.rem(xl + u, 2) * 2 + cc

    def to_twin(blk, d, ch, k):
        return remote(kv.at[blk, ch], kv.at[blk, ch], cs.at[d, ch, k], cr.at[d, ch, k], twin)

    def from_twin(blk, d, k):
        for ch in range(2):
            remote(kv.at[blk, ch], kv.at[blk, ch], cs.at[d, ch, 0], cr.at[d, ch, k], twin).wait_recv()

    def landed(k, d, ch):
        s, u = k // 2 + 1, lax.rem(k, 2)
        blk = block_at(-s if d == 0 else s, u, c)
        remote(kv.at[blk, ch], kv.at[blk, ch], zs.at[d, ch, 0], zr.at[d, ch, k], z_up).wait_recv()
        return blk

    def events(k, ch, d):
        blk = landed(k, d, ch)
        it = kv.at[blk, ch]
        if d == 0:
            @pl.when(k <= 4)
            def _():
                remote(it, it, zs.at[0, ch, k + 2], zr.at[0, ch, k + 2], z_up).start()
        else:
            @pl.when(k <= 3)
            def _():
                remote(it, it, zs.at[1, ch, k + 2], zr.at[1, ch, k + 2], z_down).start()

            @pl.when(k == 5)
            def _():
                remote(it, it, zs.at[1, ch, k + 2], zr.at[1, ch, k + 2], z_down).start()
        to_twin(blk, d, ch, k).start()

    def pair_in(ch):
        remote(kvsend.at[ch], kv.at[other, ch], xs.at[ch, 0], xr.at[ch, 0], pair).wait_recv()
        ring_send(other, ch, 1)

    pair_in(0)
    events(0, 0, 0)
    events(0, 0, 1)
    pair_in(1)

    for d in range(1, 8):
        to = lax.rem(hid + d, 8)
        go(remote(
            wout.at[:, pl.ds(pl.multiple_of(to * feat, feat), feat)], wc.at[hid],
            ws.at[d], wr.at[d], at_head(to),
        ))
    def attend(blk, parts_of=(0, 1), groups=(0, 1)):
        k = jnp.concatenate([kv[blk, 0, 0], kv[blk, 1, 0]], axis=0)
        v = jnp.concatenate([kv[blk, 0, 1], kv[blk, 1, 1]], axis=0)
        kids = [ids[pl.ds(blk * 4 + j, 1), :].astype(F32) for j in range(4)]
        for qh in parts_of:
            for i in groups:
                span = pl.ds(qh * half, half)
                q = qbuf[i, span, :]
                s = lax.dot_general(q, k, (((1,), (1,)), ((), ())), preferred_element_type=F32)
                qi = qid[i, span, :]
                parts = []
                total = None
                for j in range(4):
                    e = jnp.where(kids[j] <= qi, jnp.exp2(s[:, j * 128:(j + 1) * 128]), 0.0)
                    total = e if total is None else total + e
                    parts.append(e.astype(BF))
                w = jnp.concatenate(parts, axis=1)
                oacc[i, span, :] += jnp.dot(w, v, preferred_element_type=F32)
                lacc[i, span, :] += total

    events(0, 1, 0)
    events(0, 1, 1)
    for u in range(2):
        from_twin(block_at(0, u, 1 - c), 2, u)

    def early(group, n):
        def step(i, carry):
            attend(block_at(0, i // 2, lax.rem(i + c, 2)), groups=(group,))
            return carry

        lax.fori_loop(0, n, step, 0)

    early(xl, 4)
    for ch in range(2):
        slot = qbuf.at[1 - xl, pl.ds(ch * half, half)]
        remote(qsend.at[ch], slot, xs.at[ch, 1], xr.at[ch, 1], pair).wait_recv()
    early(1 - xl, 4)

    def loop2(f):
        lax.fori_loop(0, 2, lambda i, carry: (f(i), carry)[1], 0)


    def period(p, carry):
        for ch in range(2):
            events(p, ch, 0)
            events(p, ch, 1)
        s, u = (p + 1) // 2, lax.rem(p - 1, 2)
        loop2(lambda i: attend(block_at((2 * i - 1) * s, u, c)))
        from_twin(block_at(-s, u, 1 - c), 0, p - 1)
        from_twin(block_at(s, u, 1 - c), 1, p - 1)
        loop2(lambda i: attend(block_at((2 * i - 1) * s, u, 1 - c)))
        return carry

    lax.fori_loop(1, 6, period, 0)
    loop2(lambda i: attend(block_at((2 * i - 1) * 3, 1, c)))
    for ch in range(2):
        landed(6, 0, ch)
        go(to_twin(block_at(4, 0, c), 0, ch, 6))
        landed(7, 1, ch)
        go(to_twin(block_at(4, 1, c), 1, ch, 7))
    from_twin(block_at(-3, 1, 1 - c), 0, 5)
    from_twin(block_at(3, 1, 1 - c), 1, 5)
    loop2(lambda i: attend(block_at((2 * i - 1) * 3, 1, 1 - c)))
    def attended(i, qh):
        span = pl.ds(qh * half, half)
        total = jnp.sum(lacc[i, span, :], axis=-1, keepdims=True)
        return (oacc[i, span, :] / total).astype(BF)

    def over_x(qh, step, yy, theirs):
        mine = attg.at[hx(xh, yy), qh, xl]
        go(remote(theirs, mine, os.at[qh, step, 0], orr.at[qh, step, 0], pair))
        go(remote(theirs, mine, os.at[qh, step, 1], orr.at[qh, step, 1], diag))
        go(remote(mine, mine, os.at[qh, step, 2], orr.at[qh, step, 2], x_partner))

    def from_x(qh, step, yy):
        for k, (xx, hh, dev) in enumerate(((xh, 1 - xl, pair), (1 - xh, 1 - xl, diag), (1 - xh, xl, x_partner))):
            slot = attg.at[hx(xx, yy), qh, hh]
            remote(slot, slot, os.at[qh, 0, k], orr.at[qh, step, k], dev).wait_recv()

    loop2(lambda i: attend(block_at(4, i, c), (1,)))
    from_twin(block_at(4, 0, 1 - c), 0, 6)
    from_twin(block_at(4, 1, 1 - c), 1, 7)
    loop2(lambda i: attend(block_at(4, i, 1 - c), (1,)))
    osend[y, 1] = attended(1 - xl, 1)
    attg[hid, 1, xl] = attended(xl, 1)
    theirs, ours = osend.at[y, 1], attg.at[hid, 1, xl]
    for k, dev in enumerate((y_up, y_down)):
        go(remote(theirs, theirs, ys.at[1, k], yr.at[1, k], dev))
        go(remote(ours, ours, ys.at[1, 2 + k], yr.at[1, 2 + k], dev))
    over_x(1, 0, y, theirs)

    def last(i, carry):
        attend(lax.rem(z + 4, 8) * 4 + lax.rem(xl + i, 2) * 2 + lax.rem(c + i // 2, 2), (0,))
        return carry

    lax.fori_loop(0, 4, last, 0)
    osend[y, 0] = attended(1 - xl, 0)
    attg[hid, 0, xl] = attended(xl, 0)
    over_x(0, 0, y, osend.at[y, 0])

    lo, hi = lax.rem(y + 3, 4), lax.rem(y + 1, 4)
    for k, yy in enumerate((lo, hi)):
        theirs, ours = osend.at[yy, 1], attg.at[hx(xh, yy), 1, xl]
        dev = (y_up, y_down)[k]
        remote(theirs, theirs, ys.at[1, 0], yr.at[1, k], dev).wait_recv()
        remote(ours, ours, ys.at[1, 0], yr.at[1, 2 + k], dev).wait_recv()
        it = (theirs, ours)[k]
        go(remote(it, it, ys.at[1, 4 + k], yr.at[1, 4 + k], dev))
        over_x(1, 1 + k, yy, theirs)
    slot = attg.at[hid, 0, 1 - xl]
    remote(slot, slot, os.at[0, 0, 0], orr.at[0, 0, 0], pair).wait_recv()
    whole = attg.at[hid, 0]
    go(remote(whole, whole, ys.at[0, 0], yr.at[0, 0], y_up))
    go(remote(whole, whole, ys.at[0, 1], yr.at[0, 1], y_down))
    slot = attg.at[oid, 0, 1 - xl]
    remote(slot, slot, os.at[0, 0, 1], orr.at[0, 0, 1], diag).wait_recv()
    slot = attg.at[oid, 0, xl]
    remote(slot, slot, os.at[0, 0, 2], orr.at[0, 0, 2], x_partner).wait_recv()
    whole = attg.at[oid, 0]
    go(remote(whole, whole, ys.at[0, 2], yr.at[0, 2], y_up))
    go(remote(whole, whole, ys.at[0, 3], yr.at[0, 3], y_down))

    own_w.wait()
    for d in range(1, 8):
        frm = lax.rem(hid - d + 8, 8)
        remote(wc.at[frm], wc.at[frm], ws.at[d], wr.at[d], at_head(frm)).wait_recv()

    fin = acc3.at[:, pl.ds(0, feat)]
    fin[...] = jnp.zeros((rows, feat), F32)

    def finish(stage, qh):
        def step(i, carry):
            p = piece_of(stage, i)
            a = jnp.concatenate([attg[p, qh, 0], attg[p, qh, 1]], axis=1)
            fin[pl.ds(qh * half, half), :] += jnp.dot(a, wc[p], preferred_element_type=F32)
            return carry

        lax.fori_loop(0, 2, step, 0)

    finish(0, 0)

    def pass_half(g):
        xx = xh if g == 0 else 1 - xh
        lo, hi = attg.at[hx(xx, y - 1), 0], attg.at[hx(xx, y + 1), 0]
        remote(lo, lo, ys.at[0, 0], yr.at[0, 2 * g], y_up).wait_recv()
        go(remote(lo.at[0], lo.at[0], ys.at[0, 4 + 2 * g], yr.at[0, 4 + 2 * g], y_up))
        remote(hi, hi, ys.at[0, 1], yr.at[0, 2 * g + 1], y_down).wait_recv()
        go(remote(hi.at[1], hi.at[1], ys.at[0, 5 + 2 * g], yr.at[0, 5 + 2 * g], y_down))
        finish(1 + g, 0)

    far = lax.rem(y + 2, 4)
    theirs, ours = osend.at[far, 1], attg.at[hx(xh, far), 1, xl]
    remote(theirs, theirs, ys.at[1, 0], yr.at[1, 4], y_up).wait_recv()
    remote(ours, ours, ys.at[1, 0], yr.at[1, 5], y_down).wait_recv()
    over_x(1, 3, far, theirs)
    pass_half(0)
    pass_half(1)
    from_x(1, 0, y)
    finish(0, 1)
    from_x(1, 1, lo)
    from_x(1, 2, hi)
    finish(1, 1)
    finish(2, 1)
    for g, xx in ((0, xh), (1, 1 - xh)):
        piece = attg.at[hx(xx, y + 2), 0]
        remote(piece.at[0], piece.at[0], ys.at[0, 4], yr.at[0, 4 + 2 * g], y_up).wait_recv()
        remote(piece.at[1], piece.at[1], ys.at[0, 5], yr.at[0, 5 + 2 * g], y_down).wait_recv()
    finish(3, 0)
    from_x(1, 3, far)
    finish(3, 1)
    out[...] = fin[...].astype(BF)

    it = kv.at[0, 0]
    for ch in range(2):
        for k in range(2, 7):
            remote(it, it, zs.at[0, ch, k], zr.at[0, 0, 0], z_up).wait_send()
        for k in (2, 3, 4, 5, 7):
            remote(it, it, zs.at[1, ch, k], zr.at[1, 0, 0], z_down).wait_send()
        for k in range(6):
            for d in range(2):
                remote(it, it, cs.at[d, ch, k], cr.at[d, 0, 0], twin).wait_send()
    for copy in pending:
        copy.wait_send()


def body(tokens, norm_gain, w_qkv, head_scale, w_out, scale_ids):
    rows, feat = tokens.shape
    dim = w_qkv.shape[1]
    dma = pltpu.SemaphoreType.DMA
    any_spec = pl.BlockSpec(memory_space=pl.ANY)
    vm = pl.BlockSpec(memory_space=pltpu.VMEM)
    return pl.pallas_call(
        kernel,
        name="branch",
        out_shape=jax.ShapeDtypeStruct((rows, feat), BF),
        in_specs=[any_spec, vm, any_spec, pl.BlockSpec(memory_space=pltpu.SMEM), any_spec, vm],
        out_specs=vm,
        scratch_shapes=[
            pltpu.VMEM((8, rows, feat), BF),
            pltpu.VMEM((3, dim, feat), BF),
            pltpu.VMEM((rows, 3 * feat), F32),
            pltpu.VMEM((rows, 128), F32),
            pltpu.VMEM((32, 2, 2, rows // 2, 128), BF),
            pltpu.VMEM((2, 2, rows // 2, 128), BF),
            pltpu.VMEM((2, rows, 128), BF),
            pltpu.VMEM((2, rows // 2, 128), BF),
            pltpu.VMEM((2, rows, 128), F32),
            pltpu.VMEM((2, rows, 128), F32),
            pltpu.VMEM((2, rows, 128), F32),
            pltpu.VMEM((8, 2, 2, rows // 2, 128), BF),
            pltpu.VMEM((4, 2, rows // 2, 128), BF),
            pltpu.VMEM((8, feat, feat), BF),
            dma((3,)),
            dma((2, 4)), dma((2, 4)), dma((2, 8)), dma((2, 8)),
            dma((2, 4, 3)), dma((2, 4, 3)), dma((2, 8)), dma((2, 8)),
            dma((8,)), dma((8,)),
            dma((2, 2)), dma((2, 2)),
            dma((2, 2, 8)), dma((2, 2, 8)),
            dma((3, 2, 8)), dma((3, 2, 8)),
        ],
        compiler_params=pltpu.CompilerParams(
            collective_id=0, has_side_effects=True, vmem_limit_bytes=56 * 1024 * 1024,
        ),
        cost_estimate=pl.CostEstimate(flops=11_000_000_000, bytes_accessed=6_000_000, transcendentals=17_000_000),
    )(tokens, norm_gain.reshape(1, -1), w_qkv, head_scale.reshape(1, -1), w_out, scale_ids.reshape(-1, 128))


def solution(mesh):
    placed = (P("seq", "head"), P(), P(None, None, "head"), P("head"), P("head", None), P())
    return jax.shard_map(
        body, mesh=mesh, in_specs=placed, out_specs=P("seq", "head"), check_vma=False
    )
```
